128 devices in a mesh: seq: 32 (over y, x, core), exp: 4 (over z).
Axes of the slice: x: 4, y: 4, z: 4, core: 2. Of those that a mesh axis runs over, the one named last changes fastest.
Arguments:
- qk_proj: bfloat16 [4096, 2, 2048], P('seq', None, 'exp'), may hold values from -6 to 6
- v_proj: bfloat16 [4096, 4096], P('seq', 'exp'), may hold values from -6 to 6
- z_proj: bfloat16 [4096, 4096], P('seq', 'exp'), may hold values from -6 to 6
- conv_qk: float32 [4, 2, 2048], P(None, None, 'exp'), may hold values from -3 to 3
- conv_v: float32 [4, 4096], P(None, 'exp'), may hold values from -3 to 3
- decay_log: float32 [32, 4096], P('exp', 'seq'), may hold values from -2 to 0
- beta_gate: float32 [32, 4096], P('exp', 'seq'), may hold values from 0.05 to 0.95
- doc_ids: int32 [4096], replicated, may hold values from 0 to 31, never falling along the last dimension, each value on 1 to 1024 neighbouring positions
- head_gain: float32 [128], replicated, may hold values from 0.1 to 1.9
- out_weight: bfloat16 [4096, 2048], P('exp'), may hold values from -0.09375 to 0.09375
- residual: bfloat16 [4096, 2048], P(('seq', 'exp')), may hold values from -6 to 6
- post_gain: float32 [2048], replicated, may hold values from 0.1 to 1.9
- route_ids: int32 [4096, 10], P(('seq', 'exp')), may hold values from 0 to 255, all different within a row; in each aligned block of 32 rows (0 to 31, 32 to 63, ...) at most 2 rows name the same one
- route_weight: float32 [4096, 10], P(('seq', 'exp')), may hold values from 0.02 to 0.3
- expert_gate_up: bfloat16 [256, 2, 2048, 512], P(('seq', 'exp')), may hold values from -0.125 to 0.125
- expert_down: bfloat16 [256, 512, 2048], P(('seq', 'exp')), may hold values from -0.25 to 0.25
- shared_gate_up: bfloat16 [2, 2048, 512], replicated, may hold values from -0.125 to 0.125
- shared_down: bfloat16 [512, 2048], replicated, may hold values from -0.25 to 0.25
- shared_gate: float32 [2048], replicated, may hold values from -0.125 to 0.125
Outputs:
- hidden_mid: bfloat16 [4096, 2048], P(('seq', 'exp'))
- moe_out: bfloat16 [4096, 2048], P(('seq', 'exp'))
The draws below stay inside these ranges and needn't reach their ends.
Inputs may be any that keep to these rules, and one draw needn't show every extreme that they name: `route_ids`: each row names 10 different experts. In each aligned block of 32 rows (the rows of one device) no expert is named by more than 2 rows, and in some blocks an expert is named by exactly 2 rows. `doc_ids`: document numbers never fall along the stream; each document covers 1 to 1024 tokens, and one covers exactly 1024.
All inputs are finite; a program needn't handle non-finite values.
Results may differ from the reference program's by a relative error of at most 0.0075.
Values may be sent and summed in bfloat16 or wider, within the bound.
No kernel may reach another device: no remote copies, remote signals or barrier semaphores. Data moves between devices by JAX's collectives and lax.ppermute only.
A program may use at most 128 MiB of HBM per device.

```python
import math
import jax
import jax.numpy as jnp
import numpy as np
from jax import lax

D = 2048
VALUE_HEADS = 32
DV = 128
KCONV = 4
GROUP = 64
EFF = 512
EFF_SH = 512
TOPK = 10
TOK_DEV = 128
STREAM_TOKENS = 4096
KEYS = 2048
VALS = 4096
EXPERTS = 256
ROWS_DEV = 32
CAP = 2
DOCS = 32
DOC_MOST = 1024
N_EXP = 4


def draw_decay_log(key, part):
    key_sequence = jax.random.split(key, 7)
    fast_share = 0.5
    chooser = jax.random.uniform(key_sequence[0], (VALUE_HEADS, 1))
    fast_rate = jnp.exp(jax.random.uniform(key_sequence[1], (VALUE_HEADS, 1), minval=math.log(math.log(10.0) / 50.0), maxval=math.log(math.log(10.0) / 30.0)))
    slow_total = jnp.exp(jax.random.uniform(key_sequence[2], (VALUE_HEADS, 1), minval=math.log(0.02), maxval=math.log(0.3)))
    slow_rate = slow_total / STREAM_TOKENS
    device_count = STREAM_TOKENS // TOK_DEV
    window_len = min(32, TOK_DEV // 2)
    window_start = jax.random.randint(key_sequence[6], (VALUE_HEADS, device_count), 0, TOK_DEV - window_len + 1)
    token_position = jnp.arange(STREAM_TOKENS)
    token_offset = token_position % TOK_DEV
    start_per_token = jnp.repeat(window_start, TOK_DEV, axis=1)
    inside_window = (token_offset[None, :] >= start_per_token) & (token_offset[None, :] < start_per_token + window_len)
    baseline_rate = jnp.where((chooser < fast_share) & inside_window, fast_rate, slow_rate)
    jaggedness = jnp.exp(jax.random.uniform(key_sequence[3], (VALUE_HEADS, STREAM_TOKENS), minval=math.log(0.5), maxval=math.log(2.0)))
    spike_position = jax.random.randint(key_sequence[4], (VALUE_HEADS, 2), 0, STREAM_TOKENS)
    spike_length = jax.random.uniform(key_sequence[5], (VALUE_HEADS, 2), minval=0.22, maxval=0.69)
    spike_penalty = jnp.sum(jnp.where(token_position[None, :, None] == spike_position[:, None, :], spike_length[:, None, :], 0.0), axis=2)
    return (-(baseline_rate * jaggedness + spike_penalty)).astype(jnp.float32)


def levels(key, extent, shards, low, top_value):
    def one(position, blocks):
        draws = jax.random.uniform(jax.random.fold_in(jax.random.fold_in(key, 6), position), (blocks,), jnp.float32, low / len(shards), top_value / len(shards))
        return jnp.repeat(jnp.exp(draws), extent[position] // blocks).reshape((-1,) + (1,) * (len(extent) - position - 1))

    factor_of = one(*shards[0])
    for cut in shards[1:]:
        factor_of = factor_of * one(*cut)
    return factor_of


def length_profile(amount, total, limit, lean):
    loads = [(1 << 20) // math.isqrt(rank ** lean) + 1 for rank in range(2, amount + 1)]
    spare, given = total - limit - (amount - 1), [1] * (amount - 1)
    while spare > 0:
        free = [i for i in range(amount - 1) if given[i] < limit]
        mass, left = sum([loads[i] for i in free]), spare
        for i in free:
            more = min(limit - given[i], max(1, left * loads[i] // mass), spare)
            given[i] = given[i] + more
            spare = spare - more
    return np.array([limit] + given)


def ragged_sizes(key, amount, total, bound, slope):
    if amount == 2:
        one = jax.random.randint(key, (), max(1, total - bound), min(bound, total - 1) + 1)
        return jnp.stack([one, total - one])
    sizes = jnp.asarray(length_profile(amount, total, bound, slope), jnp.int32)
    couples = (amount - 1) // 2
    donor, taker = sizes[1:1 + 2 * couples:2], sizes[2:2 + 2 * couples:2]
    slack = jnp.minimum(donor - 1, bound - taker)
    passed = jax.random.randint(jax.random.fold_in(key, 1), (couples,), 0, 1 << 20) % (slack + 1)
    sizes = sizes.at[1:1 + 2 * couples:2].set(donor - passed).at[2:2 + 2 * couples:2].set(taker + passed)
    return sizes[jax.random.permutation(jax.random.fold_in(key, 2), amount)]


def routed_block(own_key, own, number, rows, count, top, most, lean):
    order = jax.random.permutation(own_key, count)
    packed, usual = load_shares(count, rows * top, most, lean, True), load_shares(count, rows * top, most, lean, False)
    places = jnp.arange(count)

    def named(tallies, rotation):
        used = int((tallies > 0).sum())
        fixed = max(1, used // 4)
        passed = fixed + (places - fixed + rotation * (used - fixed)) % max(1, count - fixed)
        return jnp.zeros((count,), jnp.int32).at[order[jnp.where(places < fixed, places, passed)]].set(jnp.asarray(tallies, jnp.int32))

    tallies = jnp.where(number % 4 == 0, named(packed, number // 4), named(usual, number - number // 4 - 1))
    mixed = jax.random.permutation(jax.random.fold_in(own, 3), count)
    donor, sink = mixed[0:count // 2 * 2:2], mixed[1:count // 2 * 2:2]
    margin = jnp.minimum(tallies[donor] - 1, most - tallies[sink]) // 2
    margin = jnp.where((donor == order[0]) | (sink == order[0]) | (tallies[sink] == 0), 0, jnp.maximum(margin, 0))
    passed = jax.random.randint(jax.random.fold_in(own, 4), (count // 2,), 0, 1 << 20) % (margin + 1)
    tallies = tallies.at[donor].add(-passed).at[sink].add(passed)
    labels = jnp.searchsorted(jnp.cumsum(tallies), jnp.arange(rows * top), side="right").astype(jnp.int32)
    table = labels.reshape(top, rows).T
    table = table[jax.random.permutation(jax.random.fold_in(own, 1), rows)]
    rotation = jax.random.randint(jax.random.fold_in(own, 2), (rows, 1), 0, top)
    return jnp.take_along_axis(table, (jnp.arange(top)[None, :] + rotation) % top, axis=1)


def load_shares(amount, total, limit, lean, full):
    weights = [(1 << 20) // math.isqrt(standing ** lean) + 1 for standing in range(1, amount + 1)]
    largest = limit if full else min(limit, max(-(-total // amount), total * weights[0] // sum(weights)))
    least = 1 if total - largest >= amount - 1 else 0
    holding, rest = [largest] + [least] * (amount - 1), total - largest - least * (amount - 1)
    while rest > 0:
        free = [i for i in range(1, amount) if holding[i] < largest] or [i for i in range(1, amount) if holding[i] < limit]
        pool, left = sum([weights[i] for i in free]), rest
        for i in free:
            extra = min(limit - holding[i], max(1, left * weights[i] // pool), rest)
            holding[i] = holding[i] + extra
            rest = rest - extra
    return np.array(holding)


def centred(stream_key, extent, width, limit, cuts=(), held_as=jnp.bfloat16):
    entries = jax.random.normal(stream_key, extent, jnp.float32) * width
    if len(cuts) > 0:
        entries = levels(stream_key, extent, cuts, -0.22, 0.18) * entries
    return jnp.clip(entries, min=-limit, max=limit).astype(held_as)


def setup_inputs(seed: int = 0) -> dict:
    key_list = jax.random.split(jax.random.key(seed), 20)
    qk_proj = centred(key_list[0], (STREAM_TOKENS, 2, KEYS), 1.0, 6.0, ((0, 32), (2, 4)))
    v_proj = centred(key_list[1], (STREAM_TOKENS, VALS), 1.0, 6.0, ((0, 32), (1, 4)))
    z_proj = centred(key_list[2], (STREAM_TOKENS, VALS), 1.0, 6.0, ((0, 32), (1, 4)))
    conv_qk = centred(key_list[3], (KCONV, 2, KEYS), KCONV ** -0.5, 3.0, ((2, 4),), jnp.float32)
    conv_v = centred(key_list[4], (KCONV, VALS), KCONV ** -0.5, 3.0, ((1, 4),), jnp.float32)
    decay_log = draw_decay_log(jax.random.fold_in(key_list[19], 71), 0)
    beta_gate = jnp.clip(0.05 + 0.9 * jax.random.uniform(key_list[6], (VALUE_HEADS, STREAM_TOKENS), jnp.float32) ** levels(key_list[6], (VALUE_HEADS, STREAM_TOKENS), ((0, 4), (1, 32)), -0.2, 0.2), 0.05, 0.95)
    doc_ids = jnp.searchsorted(jnp.cumsum(ragged_sizes(key_list[7], DOCS, STREAM_TOKENS, DOC_MOST, 1)), jnp.arange(STREAM_TOKENS), side="right").astype(jnp.int32)
    head_gain = jnp.clip(1.0 + 0.18 * jax.random.normal(key_list[8], (DV,), jnp.float32), 0.1, 1.9)
    out_weight = centred(key_list[9], (VALS, D), VALS ** -0.5, 0.09375, ((0, 4),))
    residual = centred(key_list[10], (STREAM_TOKENS, D), 1.0, 6.0, ((0, 128),))
    post_gain = jnp.clip(1.0 + 0.18 * jax.random.normal(key_list[11], (D,), jnp.float32), 0.1, 1.9)
    route_ids_keys = jax.random.split(jax.random.fold_in(key_list[12], 1), STREAM_TOKENS // ROWS_DEV)
    route_ids_turns = jax.random.permutation(jax.random.fold_in(key_list[12], 3), STREAM_TOKENS // ROWS_DEV)
    route_ids = jax.vmap(lambda own, number: routed_block(jax.random.fold_in(key_list[12], 2), own, number, ROWS_DEV, EXPERTS, TOPK, CAP, 2))(route_ids_keys, route_ids_turns).reshape((STREAM_TOKENS, TOPK))
    route_weight = jnp.clip(jnp.exp(math.log(0.3) - 2.7080503 * jax.random.uniform(key_list[13], (STREAM_TOKENS, TOPK), jnp.float32) ** levels(key_list[13], (STREAM_TOKENS, TOPK), ((0, 128),), -0.2, 0.2)), 0.02, 0.3)
    expert_gate_up = centred(key_list[14], (EXPERTS, 2, D, EFF), D ** -0.5, 0.125, ((0, 128),))
    expert_down = centred(key_list[15], (EXPERTS, EFF, D), EFF ** -0.5, 0.25, ((0, 128),))
    shared_gate_up = centred(key_list[16], (2, D, EFF_SH), D ** -0.5, 0.125)
    shared_down = centred(key_list[17], (EFF_SH, D), EFF_SH ** -0.5, 0.25)
    shared_gate = centred(key_list[18], (D,), D ** -0.5, 0.125, (), jnp.float32)
    return dict(qk_proj=qk_proj, v_proj=v_proj, z_proj=z_proj, conv_qk=conv_qk, conv_v=conv_v, decay_log=decay_log, beta_gate=beta_gate, doc_ids=doc_ids, head_gain=head_gain, out_weight=out_weight, residual=residual, post_gain=post_gain, route_ids=route_ids, route_weight=route_weight, expert_gate_up=expert_gate_up, expert_down=expert_down, shared_gate_up=shared_gate_up, shared_down=shared_down, shared_gate=shared_gate)


exact_result = lax.Precision.HIGHEST

def causal_conv(extended, weight, doc_window):
    kernel_len = weight.shape[0]
    length = extended.shape[0] - kernel_len + 1
    own_doc = doc_window[kernel_len - 1:]
    summed = jnp.zeros((length,) + extended.shape[1:], jnp.float32)
    for tap_index in range(kernel_len):
        same_doc = (doc_window[tap_index:tap_index + length] == own_doc).astype(jnp.float32)
        same_doc = same_doc.reshape((length,) + (1,) * (extended.ndim - 1))
        summed = summed + weight[tap_index] * (extended[tap_index:tap_index + length].astype(jnp.float32) * same_doc)
    return jax.nn.silu(summed)

def prepare(qk_conv, v_conv, decay_log, beta_gate, doc_window, block_len):
    length = v_conv.shape[0]
    head_count = decay_log.shape[0]
    key_heads = head_count // 2
    key_dim = qk_conv.shape[2] // key_heads
    value_dim = v_conv.shape[1] // head_count
    split_qk = qk_conv.reshape(length, 2, key_heads, key_dim)
    unit_qk = split_qk * lax.rsqrt(lax.optimization_barrier(jnp.sum(split_qk * split_qk, axis=-1, keepdims=True)) + 1e-06)
    blocks = length // block_len

    def heads_first(tensor):
        return jnp.transpose(tensor, (1, 0, 2)).reshape(head_count, blocks, block_len, tensor.shape[2])
    queries = heads_first(jnp.repeat(unit_qk[:, 0], 2, axis=1) * key_dim ** (-0.5))
    key_vecs = heads_first(jnp.repeat(unit_qk[:, 1], 2, axis=1))
    values = heads_first(v_conv.reshape(length, head_count, value_dim))
    decays = decay_log.reshape(head_count, blocks, block_len)
    rates = beta_gate.reshape(head_count, blocks, block_len)
    kernel_len = doc_window.shape[0] - length + 1
    seg_block = doc_window[kernel_len - 1:].reshape(blocks, block_len)
    seg_before = doc_window[kernel_len - 2:kernel_len - 2 + length:block_len]
    return (queries, key_vecs, values, decays, rates, seg_block, seg_before)

def delta_blocks(queries, key_vecs, values, decays, rates, seg_block, seg_before):
    block_len = key_vecs.shape[2]
    value_dim = values.shape[3]
    cum_decay = jnp.cumsum(decays, axis=-1)
    lower_incl = jnp.tril(jnp.ones((block_len, block_len), dtype=bool))
    strict_lower = jnp.tril(jnp.ones((block_len, block_len), dtype=bool), -1)
    same_doc = seg_block[:, :, None] == seg_block[:, None, :]
    keep_mask = same_doc & lower_incl
    spread = cum_decay[..., :, None] - cum_decay[..., None, :]
    within = jnp.exp(jnp.where(keep_mask, spread, 0.0)) * keep_mask
    carried = jnp.exp(cum_decay) * (seg_block == seg_before[:, None])
    key_dots = jnp.einsum('hnik,hnjk->hnij', key_vecs, key_vecs, precision=exact_result)
    system = jnp.eye(block_len, dtype=jnp.float32) + rates[..., :, None] * within * key_dots * strict_lower
    right_sides = jnp.concatenate([rates[..., None] * values, (rates * carried)[..., None] * key_vecs], axis=-1)
    solved = jax.scipy.linalg.solve_triangular(system, right_sides, lower=True, unit_diagonal=True)
    new_values = solved[..., :value_dim]
    key_weights = solved[..., value_dim:]
    scores = jnp.einsum('hnik,hnjk->hnij', queries, key_vecs, precision=exact_result) * within
    out_local = jnp.einsum('hnij,hnjv->hniv', scores, new_values, precision=exact_result)
    query_eff = carried[..., None] * queries - jnp.einsum('hnij,hnjk->hnik', scores, key_weights, precision=exact_result)
    end_keys = within[..., -1, :][..., None] * key_vecs
    transit = carried[..., -1][..., None, None] * jnp.eye(key_vecs.shape[3], dtype=jnp.float32) - jnp.einsum('hnjk,hnjl->hnkl', end_keys, key_weights, precision=exact_result)
    offset = jnp.einsum('hnjk,hnjv->hnkv', end_keys, new_values, precision=exact_result)
    return (out_local, query_eff, transit, offset)

def run_blocks(query_eff, out_local, transit, offset, start_state):

    def advance(current_state, pieces):
        effective_query, local_output, permute_matrix, beta_matrix = pieces
        layer_output = jnp.einsum('mjw,mwq->mjq', effective_query, current_state, precision=exact_result) + local_output
        following_state = jnp.einsum('jyu,jug->jyg', permute_matrix, current_state, precision=exact_result) + beta_matrix
        return (following_state, layer_output)
    stacked = (jnp.moveaxis(query_eff, 1, 0), jnp.moveaxis(out_local, 1, 0), jnp.moveaxis(transit, 1, 0), jnp.moveaxis(offset, 1, 0))
    last_state, outputs = lax.scan(advance, start_state, stacked)
    return outputs

def gated_norm(outputs, z_proj, head_gain):
    blocks, head_count, block_len, value_dim = outputs.shape
    attn_heads = jnp.transpose(outputs, (0, 2, 1, 3)).reshape(blocks * block_len, head_count, value_dim)
    gate_z = z_proj.reshape(blocks * block_len, head_count, value_dim).astype(jnp.float32)
    scaled = attn_heads * lax.rsqrt(lax.optimization_barrier(jnp.mean(attn_heads * attn_heads, axis=-1, keepdims=True)) + 1e-06) * head_gain * jax.nn.silu(gate_z)
    return scaled.reshape(blocks * block_len, head_count * value_dim).astype(jnp.bfloat16)

def rms_scale(hidden, gain):
    return (hidden * lax.rsqrt(lax.optimization_barrier(jnp.mean(hidden * hidden, axis=-1, keepdims=True)) + 1e-06) * gain).astype(jnp.bfloat16)

def reference(qk_proj, v_proj, z_proj, conv_qk, conv_v, decay_log, beta_gate, doc_ids, head_gain, out_weight, residual, post_gain, route_ids, route_weight, expert_gate_up, expert_down, shared_gate_up, shared_down, shared_gate):
    kernel_len = conv_qk.shape[0]
    doc_window = jnp.concatenate([jnp.full((kernel_len - 1,), -1, jnp.int32), doc_ids.astype(jnp.int32)])
    qk_ext = jnp.concatenate([jnp.zeros((kernel_len - 1,) + qk_proj.shape[1:], qk_proj.dtype), qk_proj], axis=0)
    v_ext = jnp.concatenate([jnp.zeros((kernel_len - 1,) + v_proj.shape[1:], v_proj.dtype), v_proj], axis=0)
    qk_conv = causal_conv(qk_ext, conv_qk, doc_window)
    v_conv = causal_conv(v_ext, conv_v, doc_window)
    queries, key_vecs, values, decays, rates, seg_block, seg_before = prepare(qk_conv, v_conv, decay_log, beta_gate, doc_window, GROUP)
    out_local, query_eff, transit, offset = delta_blocks(queries, key_vecs, values, decays, rates, seg_block, seg_before)
    start_state = jnp.zeros((transit.shape[0], transit.shape[2], offset.shape[3]), jnp.float32)
    outputs = run_blocks(query_eff, out_local, transit, offset, start_state)
    gated = gated_norm(outputs, z_proj, head_gain)
    hidden = residual.astype(jnp.float32) + jnp.dot(gated.astype(jnp.float32), out_weight.astype(jnp.float32), preferred_element_type=jnp.float32)
    normed = rms_scale(hidden, post_gain)
    model_width = normed.shape[1]
    block_rows = TOK_DEV // N_EXP
    block_count = STREAM_TOKENS // block_rows
    pair_count = block_rows * TOPK
    pair_index = jnp.arange(pair_count, dtype=jnp.int32)

    def block_rank(block_ids):
        earlier = (block_ids[:, None] == block_ids[None, :]) & (pair_index[None, :] < pair_index[:, None])
        return lax.optimization_barrier(jnp.sum(earlier.astype(jnp.int32), axis=1))
    slot_rank = lax.map(block_rank, route_ids.reshape(block_count, pair_count)).reshape(-1)
    flat_ids = route_ids.reshape(-1)
    all_pairs = jnp.arange(STREAM_TOKENS * TOPK, dtype=jnp.int32)
    column = all_pairs // pair_count * CAP + slot_rank
    slot_table = jnp.full((EXPERTS, block_count * CAP), STREAM_TOKENS, jnp.int32).at[flat_ids, column].set(all_pairs // TOPK)
    padded_in = jnp.concatenate([normed, jnp.zeros((1, model_width), normed.dtype)], axis=0)

    def one_expert(pieces):
        slot_rows, gate_up, down_rows = pieces
        rows_in = padded_in[slot_rows]
        gate_half = jnp.dot(rows_in.astype(jnp.float32), gate_up[0].astype(jnp.float32), preferred_element_type=jnp.float32)
        up_half = jnp.dot(rows_in.astype(jnp.float32), gate_up[1].astype(jnp.float32), preferred_element_type=jnp.float32)
        activated = (jax.nn.silu(gate_half) * up_half).astype(jnp.bfloat16)
        return jnp.dot(activated.astype(jnp.float32), down_rows.astype(jnp.float32), preferred_element_type=jnp.float32).astype(jnp.bfloat16)
    expert_out = lax.map(one_expert, (slot_table, expert_gate_up, expert_down))
    picked = expert_out[flat_ids, column].reshape(STREAM_TOKENS, TOPK, model_width)
    weighted = lax.optimization_barrier(jnp.sum(route_weight[..., None] * picked.astype(jnp.float32), axis=1))
    shared_gate_half = jnp.dot(normed.astype(jnp.float32), shared_gate_up[0].astype(jnp.float32), preferred_element_type=jnp.float32)
    shared_up_half = jnp.dot(normed.astype(jnp.float32), shared_gate_up[1].astype(jnp.float32), preferred_element_type=jnp.float32)
    shared_act = (jax.nn.silu(shared_gate_half) * shared_up_half).astype(jnp.bfloat16)
    shared_branch = jnp.dot(shared_act.astype(jnp.float32), shared_down.astype(jnp.float32), preferred_element_type=jnp.float32)
    shared_scale = jax.nn.sigmoid(jnp.dot(normed.astype(jnp.float32), shared_gate, precision=exact_result))
    moe_sum = weighted + shared_scale[:, None] * shared_branch
    return (hidden.astype(jnp.bfloat16), moe_sum.astype(jnp.bfloat16))
```

```python
import functools

import jax
import jax.numpy as jnp
from jax import lax
from jax.experimental import pallas as pl
from jax.experimental.pallas import tpu as pltpu
from jax.sharding import PartitionSpec as P

F32 = jnp.float32
BF16 = jnp.bfloat16
HIGH = lax.Precision.HIGHEST
L = 128
HD = 128
HEADS = 8
RUN = 8
VMEM_CAP = 40 * 1024 * 1024


def dotf(a, b, ca=1, cb=0):
    return lax.dot_general(a, b, (((ca,), (cb,)), ((), ())), precision=HIGH, preferred_element_type=F32)


def dotb(a, b, ca=1, cb=0):
    return lax.dot_general(a, b, (((ca,), (cb,)), ((), ())), preferred_element_type=F32)


def split(x):
    hi = x.astype(BF16)
    return hi, (x - hi.astype(F32)).astype(BF16)


def silu(x):
    return x * jax.nn.sigmoid(x)


def call(body, outs, *args, scratch=(), specs=None, flops=0, name=None):
    vmem = pl.BlockSpec(memory_space=pltpu.VMEM)
    size = sum(a.size * a.dtype.itemsize for a in args)
    return pl.pallas_call(
        body,
        out_shape=outs,
        in_specs=specs or [vmem] * len(args),
        out_specs=jax.tree.map(lambda _: vmem, outs),
        scratch_shapes=list(scratch),
        compiler_params=pltpu.CompilerParams(vmem_limit_bytes=VMEM_CAP),
        cost_estimate=pl.CostEstimate(flops=flops, bytes_accessed=size, transcendentals=0),
        name=name,
    )(*args)


def sds(shape, dtype):
    return jax.ShapeDtypeStruct(shape, dtype)


def iota(shape, dim):
    return lax.broadcasted_iota(jnp.int32, shape, dim)


def conv(x_ref, halo, taps, same_cols):
    x = x_ref[...].astype(F32)
    width = x.shape[1]
    row8 = iota((8, width), 0)
    total = taps(3) * x
    for s in (1, 2, 3):
        moved = pltpu.roll(x, s, 0)
        first = jnp.where(row8 < s, pltpu.roll(halo, s, 0), moved[:8])
        moved = jnp.concatenate([first, moved[8:]], axis=0)
        total = total + taps(3 - s) * (moved * same_cols[s - 1])
    return silu(total)


def maps_kernel(q_ref, k_ref, v_ref, halo_ref, cqk_ref, cv_ref, decay_ref, beta_ref, doc_ref, maps_ref, sc_ref, uw_ref, cq_ref):
    me = lax.axis_index("seq")
    cur = doc_ref[pl.ds(me, 1), :]
    prev = doc_ref[pl.ds(jnp.maximum(me - 1, 0), 1), :]
    prev = jnp.where(me == 0, -1, prev)
    cur8 = jnp.broadcast_to(cur, (8, L)).astype(F32)
    prev8 = jnp.broadcast_to(prev, (8, L)).astype(F32)
    lane8 = iota((8, L), 1)
    row8 = iota((8, L), 0)
    cum = decay_ref[...]
    for step in (1, 2, 4, 8, 16, 32, 64):
        cum = cum + jnp.where(lane8 >= step, pltpu.roll(cum, step, 1), 0.0)
    flags = (cur8 == prev8[:, L - 1 :]).astype(F32)
    for s in (1, 2, 3):
        shifted = jnp.where(lane8 < s, pltpu.roll(prev8, s, 1), pltpu.roll(cur8, s, 1))
        flags = jnp.where(row8 == s, (shifted == cur8).astype(F32), flags)
    flags = jnp.where(row8 == 4, cur8, flags)
    rows = jnp.concatenate([cum, beta_ref[...], flags, jnp.zeros((L - 24, L), F32)], axis=0)
    cols = rows.T
    carry_col = cols[:, 16:17]
    same_cols = [cols[:, 17:18], cols[:, 18:19], cols[:, 19:20]]
    doc_col = cols[:, 20:21]
    doc_row = cur8[:1]

    halo = halo_ref[...].astype(F32)
    kw = q_ref.shape[1]
    q = conv(q_ref, halo[:, :kw], lambda i: cqk_ref[i, 0:1, :], same_cols)
    k = conv(k_ref, halo[:, kw : 2 * kw], lambda i: cqk_ref[i, 1:2, :], same_cols)
    v = conv(v_ref, halo[:, 2 * kw :], lambda i: cv_ref[i : i + 1, :], same_cols)

    ri, ci = iota((L, L), 0), iota((L, L), 1)
    same = doc_col == doc_row
    keep = same & (ri >= ci)
    strict = ri > ci
    eye = (ri == ci).astype(F32)
    end_same = doc_col == doc_row[:, L - 1 :]
    q_heads, k_heads, kk, qk = [], [], [], []
    for j in range(HEADS // 2):
        qj, kj = q[:, j * HD : (j + 1) * HD], k[:, j * HD : (j + 1) * HD]
        qj = qj * lax.rsqrt(jnp.sum(qj * qj, axis=1, keepdims=True) + 1e-06) * (HD ** -0.5)
        kj = kj * lax.rsqrt(jnp.sum(kj * kj, axis=1, keepdims=True) + 1e-06)
        q_heads.append(qj)
        k_heads.append(kj)
        kk.append(dotf(kj, kj, 1, 1))
        qk.append(dotf(qj, kj, 1, 1))
    systems, inverses = [], []
    for h in range(HEADS):
        c_col, c_row = cols[:, h : h + 1], cum[h : h + 1]
        within = jnp.where(keep, jnp.exp(jnp.where(keep, c_col - c_row, 0.0)), 0.0)
        sc_ref[h] = qk[h // 2] * within
        systems.append(jnp.where(strict, cols[:, 8 + h : 9 + h] * within * kk[h // 2], 0.0))
    one = (ri // 2 == ci // 2)
    inverses = [eye - jnp.where(one, a, 0.0) for a in systems]
    size = 2
    while size < L:
        pick = (ri // (2 * size) == ci // (2 * size)) & (ri // size != ci // size)
        inner = [dotf(jnp.where(pick, a, 0.0), x) for a, x in zip(systems, inverses)]
        inverses = [x - dotf(x, y) for x, y in zip(inverses, inner)]
        size *= 2
    for h in range(HEADS):
        kj = k_heads[h // 2]
        c_col = cols[:, h : h + 1]
        b_col = cols[:, 8 + h : 9 + h]
        carried = jnp.exp(c_col) * carry_col
        right = jnp.concatenate([b_col * v[:, h * HD : (h + 1) * HD], (b_col * carried) * kj], axis=1)
        uw = dotf(inverses[h], right)
        uw_ref[h] = uw
        cq_ref[h] = carried * q_heads[h // 2]
        c_last = cum[h : h + 1, L - 1 :]
        end_w = jnp.where(end_same, jnp.exp(jnp.where(end_same, c_last - c_col, 0.0)), 0.0)
        ends = dotf(end_w * kj, uw, 0, 0)
        maps_ref[h, :L] = (carried[L - 1 :] * eye - ends[:, HD:]).astype(BF16)
        maps_ref[h, L:] = ends[:, :HD].astype(BF16)


def local_kernel(sc_ref, uw_ref, cq_ref, out_ref, qe_ref):
    for h in range(HEADS):
        both = dotf(sc_ref[h], uw_ref[h])
        out_ref[h] = both[:, :HD]
        hi, lo = split(cq_ref[h] - both[:, HD:])
        qe_ref[h, :, :HD] = hi
        qe_ref[h, :, HD:] = lo


def chain_kernel(maps_ref, pq_ref, end_ref):
    ri, ci = iota((HD, HD), 0), iota((HD, HD), 1)
    state = jnp.concatenate([jnp.zeros((HD, HD), F32), (ri == ci).astype(F32)], axis=1)
    for i in range(RUN):
        pq_ref[i] = state
        trans = maps_ref[i, :HD]
        offset = maps_ref[i, HD:].astype(F32)
        if i == 0:
            state = jnp.concatenate([offset, trans.astype(F32)], axis=1)
            continue
        hi, lo = split(state)
        moved = dotb(jnp.concatenate([trans, trans], axis=1), jnp.concatenate([hi, lo], axis=0))
        state = jnp.concatenate([moved[:, :HD] + offset, moved[:, HD:]], axis=1)
    end_ref[...] = state[:, :HD].astype(BF16)


def starts_kernel(pq_ref, end_ref, start_ref):
    end = end_ref[...]
    ends = jnp.concatenate([end, end], axis=0)
    for i in range(RUN):
        hi, lo = split(pq_ref[i, :, HD:])
        moved = dotb(jnp.concatenate([hi, lo], axis=1), ends)
        start_ref[i] = (pq_ref[i, :, :HD] + moved).astype(BF16)


def project_kernel(out_ref, qe_ref, start_ref, z_ref, gain_ref, w_hbm, own_ref, s1_ref, s2_ref, s3_ref, w_ref, part_ref, sem):
    pieces = 4
    rows = w_ref.shape[0] // pieces
    copies = [
        pltpu.make_async_copy(w_hbm.at[pl.ds(p * rows, rows)], w_ref.at[pl.ds(p * rows, rows)], sem.at[p])
        for p in range(pieces)
    ]
    for copy in copies:
        copy.start()
    gain = gain_ref[...]
    gated = []
    for h in range(HEADS):
        start = start_ref[h]
        attn = out_ref[h] + dotb(qe_ref[h], jnp.concatenate([start, start], axis=0))
        z = z_ref[:, h * HD : (h + 1) * HD].astype(F32)
        scale = lax.rsqrt(jnp.mean(attn * attn, axis=1, keepdims=True) + 1e-06)
        gated.append((attn * scale * gain * silu(z)).astype(BF16))
    per = HEADS // pieces
    total = None
    for p in range(pieces):
        copies[p].wait()
        left = jnp.concatenate(gated[p * per : (p + 1) * per], axis=1)
        term = dotb(left, w_ref[pl.ds(p * rows, rows)])
        total = term if total is None else total + term
    part_ref[...] = total
    me = lax.axis_index("exp")
    n = own_ref.shape[0]
    own_ref[...] = part_ref[pl.ds(pl.multiple_of(me * n, n), n)]
    for s, ref in ((1, s1_ref), (2, s2_ref), (3, s3_ref)):
        to = lax.rem(me + s, 4)
        ref[...] = part_ref[pl.ds(pl.multiple_of(to * n, n), n)].astype(BF16)


def route_kernel(own_ref, r1_ref, r2_ref, r3_ref, res_ref, gain_ref, ids_ref, wt_ref, mid_ref, norm_ref, send_ref, pick_ref):
    hidden = own_ref[...] + r1_ref[...].astype(F32) + r2_ref[...].astype(F32) + r3_ref[...].astype(F32)
    hidden = res_ref[...].astype(F32) + hidden
    mid_ref[...] = hidden.astype(BF16)
    normed = hidden * lax.rsqrt(jnp.mean(hidden * hidden, axis=1, keepdims=True) + 1e-06) * gain_ref[...]
    normed = normed.astype(BF16)
    norm_ref[...] = normed
    tokens, width = normed.shape
    half = width // 2
    slots = send_ref.shape[0]
    col = iota((tokens, slots), 1)
    expert = col // 4
    rank = (col // 2) % 2
    named = jnp.zeros((tokens, slots), F32)
    weight = jnp.zeros((tokens, slots), F32)
    for k in range(ids_ref.shape[1]):
        hit = expert == ids_ref[:, k : k + 1]
        named = jnp.where(hit, 1.0, named)
        weight = jnp.where(hit, wt_ref[:, k : k + 1], weight)
    before = (iota((tokens, tokens), 0) > iota((tokens, tokens), 1)).astype(BF16)
    earlier = dotb(before, named.astype(BF16))
    chosen = jnp.where(earlier == rank.astype(F32), named, 0.0)
    weight = chosen * weight
    low = col % 2 == 0
    pick = jnp.concatenate([jnp.where(low, chosen, 0.0), jnp.where(low, 0.0, chosen)], axis=0).astype(BF16)
    send_ref[...] = dotb(pick, jnp.concatenate([normed[:, :half], normed[:, half:]], axis=0), 0, 0).astype(BF16)
    both = jnp.concatenate([jnp.where(low, weight, 0.0), jnp.where(low, 0.0, weight)], axis=0)
    hi, lo = split(both)
    pick_ref[: 2 * tokens] = hi
    pick_ref[2 * tokens :] = lo


def shared_kernel(norm_ref, gu_ref, down_ref, gate_ref, out_ref):
    normed = norm_ref[...]
    act = (silu(dotb(normed, gu_ref[0])) * dotb(normed, gu_ref[1])).astype(BF16)
    branch = dotb(act, down_ref[...])
    score = jnp.sum(normed.astype(F32) * gate_ref[...], axis=1, keepdims=True)
    out_ref[...] = jax.nn.sigmoid(score) * branch


def expert_kernel(recv_ref, gu_hbm, down_hbm, out_ref, gu_ref, down_ref, flat_ref, x_ref, sem):
    copies = []
    for e in range(2):
        for z in range(2):
            copies.append(pltpu.make_async_copy(gu_hbm.at[e, z], gu_ref.at[e, z], sem.at[3 * e + z]))
        copies.append(pltpu.make_async_copy(down_hbm.at[e], down_ref.at[e], sem.at[3 * e + 2]))
    for copy in copies:
        copy.start()
    rows, half = recv_ref.shape
    srcs = rows // 8
    flat = functools.partial(pl.ds, size=srcs, stride=8)
    lanes = 128
    for c in range(half // lanes):
        at = slice(c * lanes, (c + 1) * lanes)
        flat_ref[c] = recv_ref[:, at].astype(F32)
        for e in range(2):
            for r in range(2):
                for b in range(2):
                    x_ref[e, r * srcs : (r + 1) * srcs, b * half + c * lanes : b * half + (c + 1) * lanes] = flat_ref[
                        c, flat(4 * e + 2 * r + b), :
                    ].astype(BF16)
    for e in range(2):
        x = x_ref[e]
        copies[3 * e].wait()
        gate = dotb(x, gu_ref[e, 0])
        copies[3 * e + 1].wait()
        act = (silu(gate) * dotb(x, gu_ref[e, 1])).astype(BF16)
        copies[3 * e + 2].wait()
        for b in range(2):
            y = dotb(act, down_ref[e, :, b * half : (b + 1) * half])
            for r in range(2):
                for c in range(half // lanes):
                    flat_ref[c, flat(4 * e + 2 * r + b), :] = y[r * srcs : (r + 1) * srcs, c * lanes : (c + 1) * lanes]
    for c in range(half // lanes):
        out_ref[:, c * lanes : (c + 1) * lanes] = flat_ref[c].astype(BF16)


def combine_kernel(back_ref, pick_ref, shared_ref, out_ref):
    got = dotb(pick_ref[...], back_ref[...])
    n = got.shape[0] // 4
    half = got.shape[1]
    got = got[: 2 * n] + got[2 * n :]
    out_ref[:, :half] = (got[:n] + shared_ref[:, :half]).astype(BF16)
    out_ref[:, half:] = (got[n:] + shared_ref[:, half:]).astype(BF16)


def shards(
    qk_proj,
    v_proj,
    z_proj,
    conv_qk,
    conv_v,
    decay_log,
    beta_gate,
    doc_ids,
    head_gain,
    out_weight,
    residual,
    post_gain,
    route_ids,
    route_weight,
    expert_gate_up,
    expert_down,
    shared_gate_up,
    shared_down,
    shared_gate,
):
    seq_n, exp_n = lax.axis_size("seq"), lax.axis_size("exp")
    runs = [[g * RUN + i for i in range(RUN)] for g in range(seq_n // RUN)]
    q, k = qk_proj[:, 0], qk_proj[:, 1]
    rim = jnp.concatenate([q[L - 8 :], k[L - 8 :], v_proj[L - 8 :]], axis=1)
    halo = lax.ppermute(rim, "seq", [(i, i + 1) for i in range(seq_n - 1)])

    maps, scores, uw, cq = call(
        maps_kernel,
        (
            sds((HEADS, 2 * HD, HD), BF16),
            sds((HEADS, L, L), F32),
            sds((HEADS, L, 2 * HD), F32),
            sds((HEADS, L, HD), F32),
        ),
        q, k, v_proj, halo, conv_qk, conv_v, decay_log, beta_gate, doc_ids.reshape(seq_n, L),
        flops=2 * 10**9,
        name="maps",
    )
    maps = lax.all_to_all(maps, "seq", split_axis=0, concat_axis=0, tiled=True, axis_index_groups=runs)
    local_out, query_eff = call(
        local_kernel,
        (sds((HEADS, L, HD), F32), sds((HEADS, L, 2 * HD), BF16)),
        scores, uw, cq,
        flops=10**8,
        name="local_out",
    )
    pq, end = call(
        chain_kernel,
        (sds((RUN, HD, 2 * HD), F32), sds((HD, HD), BF16)),
        maps,
        flops=10**8,
        name="chain",
    )
    end = lax.ppermute(end, "seq", [(i, i + RUN) for i in range(seq_n - RUN)])
    starts = call(starts_kernel, sds((RUN, HD, HD), BF16), pq, end, flops=10**8, name="starts")
    starts = lax.all_to_all(starts, "seq", split_axis=0, concat_axis=0, tiled=True, axis_index_groups=runs)

    model = out_weight.shape[1]
    rows = residual.shape[0]
    vmem, anyw = pl.BlockSpec(memory_space=pltpu.VMEM), pl.BlockSpec(memory_space=pl.ANY)
    piece = sds((rows, model), BF16)
    own, *sends = call(
        project_kernel,
        (sds((rows, model), F32), piece, piece, piece),
        local_out, query_eff, starts, z_proj, head_gain.reshape(1, HD), out_weight,
        specs=[vmem] * 5 + [anyw],
        scratch=[pltpu.VMEM(out_weight.shape, BF16), pltpu.VMEM((L, model), F32), pltpu.SemaphoreType.DMA((4,))],
        flops=6 * 10**8,
        name="project",
    )
    got = {}
    for s in (2, 1, 3):
        got[s] = lax.ppermute(sends[s - 1], "exp", [(i, (i + s) % exp_n) for i in range(exp_n)])
    devices = seq_n * exp_n
    slots = devices * 8
    half = model // 2
    hidden_mid, normed, send, pick = call(
        route_kernel,
        (piece, piece, sds((slots, half), BF16), sds((4 * rows, slots), BF16)),
        own, got[1], got[2], got[3], residual, post_gain.reshape(1, model), route_ids, route_weight,
        flops=2 * 10**8,
        name="route",
    )
    axes = ("seq", "exp")
    recv = lax.all_to_all(send.reshape(devices, 8, half), axes, split_axis=0, concat_axis=0, tiled=True)
    shared = call(
        shared_kernel,
        sds((rows, model), F32),
        normed, shared_gate_up, shared_down, shared_gate.reshape(1, model),
        flops=2 * 10**8,
        name="shared",
    )
    made = call(
        expert_kernel,
        sds((slots, half), BF16),
        recv.reshape(slots, half), expert_gate_up, expert_down,
        specs=[vmem, anyw, anyw],
        scratch=[
            pltpu.VMEM(expert_gate_up.shape, BF16),
            pltpu.VMEM(expert_down.shape, BF16),
            pltpu.VMEM((half // 128, slots, 128), F32),
            pltpu.VMEM((2, 2 * devices, model), BF16),
            pltpu.SemaphoreType.DMA((6,)),
        ],
        flops=4 * 10**9,
        name="experts",
    )
    back = lax.all_to_all(made.reshape(devices, 8, half), axes, split_axis=0, concat_axis=0, tiled=True)
    moe_out = call(
        combine_kernel,
        piece,
        back.reshape(slots, half), pick, shared,
        flops=3 * 10**8,
        name="combine",
    )
    return hidden_mid, moe_out


def solution(mesh):
    placed = (
        P("seq", None, "exp"),
        P("seq", "exp"),
        P("seq", "exp"),
        P(None, None, "exp"),
        P(None, "exp"),
        P("exp", "seq"),
        P("exp", "seq"),
        P(),
        P(),
        P("exp", None),
        P(("seq", "exp"), None),
        P(),
        P(("seq", "exp"), None),
        P(("seq", "exp"), None),
        P(("seq", "exp"), None, None, None),
        P(("seq", "exp"), None, None),
        P(),
        P(),
        P(),
    )
    return jax.shard_map(
        shards,
        mesh=mesh,
        in_specs=placed,
        out_specs=(P(("seq", "exp"), None), P(("seq", "exp"), None)),
        check_vma=False,
    )
```

```python
import functools

import jax
import jax.numpy as jnp
from jax import lax
from jax.experimental import pallas as pl
from jax.experimental.pallas import tpu as pltpu
from jax.sharding import PartitionSpec as P

F32 = jnp.float32
BF16 = jnp.bfloat16
HIGH = lax.Precision.HIGHEST
L = 128
HD = 128
HEADS = 8
RUN = 8
VMEM_CAP = 28 * 1024 * 1024


def dotf(a, b, ca=1, cb=0):
    return lax.dot_general(a, b, (((ca,), (cb,)), ((), ())), precision=HIGH, preferred_element_type=F32)


def dotb(a, b, ca=1, cb=0):
    return lax.dot_general(a, b, (((ca,), (cb,)), ((), ())), preferred_element_type=F32)


def split(x):
    hi = x.astype(BF16)
    return hi, (x - hi.astype(F32)).astype(BF16)


def silu(x):
    return x * jax.nn.sigmoid(x)


def call(body, outs, *args, scratch=(), hbm=(), vmem=(), flops=0, name=None):
    here, far_spec = pl.BlockSpec(memory_space=pltpu.VMEM), pl.BlockSpec(memory_space=pltpu.HBM)
    size = sum(a.size * a.dtype.itemsize for a in args)
    held = {i: pltpu.HBM for i in hbm} | {i: pltpu.VMEM for i in vmem}
    args = [pltpu.with_memory_space_constraint(a, held[i]) if i in held else a for i, a in enumerate(args)]
    made = pl.pallas_call(
        body,
        out_shape=[place(o.shape, o.dtype) if place else o for o, place in outs],
        in_specs=[far_spec if i in hbm else here for i in range(len(args))],
        out_specs=[far_spec if place is pltpu.HBM else here for _, place in outs],
        scratch_shapes=list(scratch),
        compiler_params=pltpu.CompilerParams(vmem_limit_bytes=VMEM_CAP),
        cost_estimate=pl.CostEstimate(flops=flops, bytes_accessed=size, transcendentals=0),
        name=name,
    )(*args)
    return made[0] if len(outs) == 1 else made


def near(shape, dtype):
    return jax.ShapeDtypeStruct(shape, dtype), pltpu.VMEM


def far(shape, dtype):
    return jax.ShapeDtypeStruct(shape, dtype), pltpu.HBM


def free(shape, dtype):
    return jax.ShapeDtypeStruct(shape, dtype), None


def iota(shape, dim):
    return lax.broadcasted_iota(jnp.int32, shape, dim)


def dot3(a, b, ca=1, cb=0):
    ah, al = split(a)
    bh, bl = split(b)
    return dotb(jnp.concatenate([ah, al, ah], axis=ca), jnp.concatenate([bh, bh, bl], axis=cb), ca, cb)


def prep_kernel(q_hbm, k_hbm, v_hbm, cqk_hbm, cv_hbm, decay_hbm, beta_hbm, doc_hbm, conv_ref, edge_ref, within_ref, sys_ref, cols_ref, x_ref, cqk_ref, cv_ref, db_ref, doc_ref, sem):
    kw = q_hbm.shape[1]
    vw = v_hbm.shape[1]
    pairs = (
        (doc_hbm, doc_ref),
        (decay_hbm, db_ref.at[0]),
        (beta_hbm, db_ref.at[1]),
        (cqk_hbm, cqk_ref),
        (cv_hbm, cv_ref),
        (q_hbm, x_ref.at[:, :kw]),
        (k_hbm, x_ref.at[:, kw : 2 * kw]),
        (v_hbm, x_ref.at[:, 2 * kw :]),
    )
    copies = [pltpu.make_async_copy(src, dst, sem.at[i]) for i, (src, dst) in enumerate(pairs)]
    for copy in copies:
        copy.start()
    for copy in copies[:3]:
        copy.wait()
    me = lax.axis_index("seq")
    cur = doc_ref[pl.ds(me, 1), :]
    prev = doc_ref[pl.ds(jnp.maximum(me - 1, 0), 1), :]
    prev = jnp.where(me == 0, -1, prev)
    cur8 = jnp.broadcast_to(cur, (8, L)).astype(F32)
    prev8 = jnp.broadcast_to(prev, (8, L)).astype(F32)
    lane8 = iota((8, L), 1)
    row8 = iota((8, L), 0)
    cum = db_ref[0]
    for step in (1, 2, 4, 8, 16, 32, 64):
        cum = cum + jnp.where(lane8 >= step, pltpu.roll(cum, step, 1), 0.0)
    flags = (cur8 == prev8[:, L - 1 :]).astype(F32)
    for s in (1, 2, 3):
        shifted = jnp.where(lane8 < s, pltpu.roll(prev8, s, 1), pltpu.roll(cur8, s, 1))
        flags = jnp.where(row8 == s, (shifted == cur8).astype(F32), flags)
    flags = jnp.where(row8 == 4, cur8, flags)
    last = L - 1
    doc_row = cur8[:1]
    end_same = cur8 == cur8[:, last:]
    carried = jnp.exp(cum) * (cur8 == prev8[:, last:]).astype(F32)
    ends = jnp.where(end_same, jnp.exp(jnp.where(end_same, cum[:, last:] - cum, 0.0)), 0.0)
    rows = jnp.concatenate([cum, db_ref[1], flags, carried, ends, jnp.zeros((L - 40, L), F32)], axis=0)
    cols = rows.T
    cols_ref[...] = cols
    doc_col = cols[:, 20:21]
    ri, ci = iota((L, L), 0), iota((L, L), 1)
    keep = (doc_col == doc_row) & (ri >= ci)
    strict = ri > ci
    for h in range(HEADS):
        spread = cols[:, h : h + 1] - cum[h : h + 1]
        within = jnp.where(keep, jnp.exp(jnp.where(keep, spread, 0.0)), 0.0)
        within_ref[h] = within
        sys_ref[h] = jnp.where(strict, cols[:, 8 + h : 9 + h] * within, 0.0)
    for copy in copies[3:]:
        copy.wait()

    def taps(i, at, half):
        if half is None:
            return cv_ref[i : i + 1, at]
        return cqk_ref[i, half : half + 1, at]

    step = 256
    for start in range(0, 2 * kw + vw, step):
        if start < 2 * kw:
            half, off = start // kw, start % kw
        else:
            half, off = None, start - 2 * kw
        at, here = slice(off, off + step), slice(start, start + step)
        x = x_ref[:, here].astype(F32)
        row = iota((8, step), 0)
        total = taps(3, at, half) * x
        for s in (1, 2, 3):
            moved = pltpu.roll(x, s, 0)
            moved = jnp.concatenate([jnp.where(row < s, 0.0, moved[:8]), moved[8:]], axis=0)
            total = total + taps(3 - s, at, half) * (moved * cols[:, 16 + s : 17 + s])
            edge_ref[8 + s : 9 + s, here] = taps(3 - s, at, half)
        edge_ref[:8, here] = total[:8]
        conv_ref[:, here] = silu(total)


def maps_kernel(conv_ref, edge_ref, halo_ref, within_ref, sys_ref, cols_ref, maps_ref, sc_ref, uw_ref, cq_ref):
    cols = cols_ref[...]
    halo = halo_ref[...].astype(F32)
    row8 = iota(halo.shape, 0)
    first = edge_ref[:8]
    for s in (1, 2, 3):
        moved = jnp.where(row8 < s, pltpu.roll(halo, s, 0), 0.0)
        first = first + edge_ref[8 + s : 9 + s] * (moved * cols[:8, 16 + s : 17 + s])
    first = silu(first)

    def feature(j):
        at = slice(j * HD, (j + 1) * HD)
        return jnp.concatenate([first[:, at], conv_ref[8:, at]], axis=0)

    ri, ci = iota((L, L), 0), iota((L, L), 1)
    eye = (ri == ci).astype(F32)
    pairs = HEADS // 2
    q_heads, k_heads, kk, qk = [], [], [], []
    for j in range(pairs):
        qj, kj = feature(j), feature(pairs + j)
        qj = qj * lax.rsqrt(jnp.sum(qj * qj, axis=1, keepdims=True) + 1e-06) * (HD ** -0.5)
        kj = kj * lax.rsqrt(jnp.sum(kj * kj, axis=1, keepdims=True) + 1e-06)
        q_heads.append(qj)
        k_heads.append(kj)
        dots = dot3(jnp.concatenate([qj, kj], axis=0), kj, 1, 1)
        qk.append(dots[:L])
        kk.append(dots[L:])
    systems = [sys_ref[h] * kk[h // 2] for h in range(HEADS)]
    narrow = [a.astype(BF16) for a in systems]
    zero = jnp.zeros((L, L), BF16)
    one = ri // 2 == ci // 2
    inverses = [eye - jnp.where(one, a, 0.0) for a in systems]
    size = 2
    while size < L:
        pick = (ri // (2 * size) == ci // (2 * size)) & (ri // size != ci // size)
        low = [x.astype(BF16) for x in inverses]
        inner = [dotb(jnp.where(pick, a, zero), x) for a, x in zip(narrow, low)]
        inverses = [x - dotb(b, y.astype(BF16)) for x, b, y in zip(inverses, low, inner)]
        size *= 2
    rests = [eye - x - dot3(a, x) for a, x in zip(systems, inverses)]
    inverses = [x + dotb(x.astype(BF16), r.astype(BF16)) for x, r in zip(inverses, rests)]
    for h in range(HEADS):
        kj = k_heads[h // 2]
        b_col = cols[:, 8 + h : 9 + h]
        carried = cols[:, 24 + h : 25 + h]
        right = jnp.concatenate([b_col * feature(2 * pairs + h), (b_col * carried) * kj], axis=1)
        uw = dot3(inverses[h], right)
        uw_ref[h] = uw
        sc_ref[h] = qk[h // 2] * within_ref[h]
        cq_ref[h] = carried * q_heads[h // 2]
        ends = dot3(cols[:, 32 + h : 33 + h] * kj, uw, 0, 0)
        maps_ref[h, :L] = (carried[L - 1 :] * eye - ends[:, HD:]).astype(BF16)
        maps_ref[h, L:] = ends[:, :HD].astype(BF16)


def local_kernel(sc_ref, uw_ref, cq_ref, out_ref, qe_ref):
    for h in range(HEADS):
        both = dot3(sc_ref[h], uw_ref[h])
        out_ref[h] = both[:, :HD]
        hi, lo = split(cq_ref[h] - both[:, HD:])
        qe_ref[h, :, :HD] = hi
        qe_ref[h, :, HD:] = lo


def chain_kernel(maps_ref, pq_ref, end_ref):
    ri, ci = iota((HD, HD), 0), iota((HD, HD), 1)
    state = jnp.concatenate([jnp.zeros((HD, HD), F32), (ri == ci).astype(F32)], axis=1)
    for i in range(RUN):
        pq_ref[i] = state
        trans = maps_ref[i, :HD]
        offset = maps_ref[i, HD:].astype(F32)
        if i == 0:
            state = jnp.concatenate([offset, trans.astype(F32)], axis=1)
            continue
        hi, lo = split(state)
        moved = dotb(jnp.concatenate([trans, trans], axis=1), jnp.concatenate([hi, lo], axis=0))
        state = jnp.concatenate([moved[:, :HD] + offset, moved[:, HD:]], axis=1)
    end_ref[...] = state[:, :HD].astype(BF16)


def starts_kernel(pq_ref, end_ref, start_ref):
    end = end_ref[...]
    ends = jnp.concatenate([end, end], axis=0)
    for i in range(RUN):
        hi, lo = split(pq_ref[i, :, HD:])
        moved = dotb(jnp.concatenate([hi, lo], axis=1), ends)
        start_ref[i] = (pq_ref[i, :, :HD] + moved).astype(BF16)


def project_kernel(out_ref, qe_ref, start_ref, z_ref, gain_ref, w_ref, own_ref, s1_ref, s2_ref, s3_ref, part_ref):
    gain = gain_ref[...]
    gated = []
    for h in range(HEADS):
        start = start_ref[h]
        attn = out_ref[h] + dotb(qe_ref[h], jnp.concatenate([start, start], axis=0))
        z = z_ref[:, h * HD : (h + 1) * HD].astype(F32)
        scale = lax.rsqrt(jnp.mean(attn * attn, axis=1, keepdims=True) + 1e-06)
        gated.append((attn * scale * gain * silu(z)).astype(BF16))
    part_ref[...] = dotb(jnp.concatenate(gated, axis=1), w_ref[...])
    me = lax.axis_index("exp")
    n = own_ref.shape[0]
    own_ref[...] = part_ref[pl.ds(pl.multiple_of(me * n, n), n)]
    for s, ref in ((1, s1_ref), (2, s2_ref), (3, s3_ref)):
        to = lax.rem(me + s, 4)
        ref[...] = part_ref[pl.ds(pl.multiple_of(to * n, n), n)].astype(BF16)


def route_kernel(own_ref, r1_ref, r2_ref, r3_ref, res_ref, gain_ref, ids_ref, wt_ref, mid_ref, norm_ref, send_ref, pick_ref):
    hidden = own_ref[...] + r1_ref[...].astype(F32) + r2_ref[...].astype(F32) + r3_ref[...].astype(F32)
    hidden = res_ref[...].astype(F32) + hidden
    mid_ref[...] = hidden.astype(BF16)
    normed = hidden * lax.rsqrt(jnp.mean(hidden * hidden, axis=1, keepdims=True) + 1e-06) * gain_ref[...]
    normed = normed.astype(BF16)
    norm_ref[...] = normed
    tokens, width = normed.shape
    half = width // 2
    slots = send_ref.shape[0]
    col = iota((tokens, slots), 1)
    expert = col // 4
    rank = (col // 2) % 2
    named = jnp.zeros((tokens, slots), F32)
    weight = jnp.zeros((tokens, slots), F32)
    for k in range(ids_ref.shape[1]):
        hit = expert == ids_ref[:, k : k + 1]
        named = jnp.where(hit, 1.0, named)
        weight = jnp.where(hit, wt_ref[:, k : k + 1], weight)
    before = (iota((tokens, tokens), 0) > iota((tokens, tokens), 1)).astype(BF16)
    earlier = dotb(before, named.astype(BF16))
    chosen = jnp.where(earlier == rank.astype(F32), named, 0.0)
    weight = chosen * weight
    low = col % 2 == 0
    pick = jnp.concatenate([jnp.where(low, chosen, 0.0), jnp.where(low, 0.0, chosen)], axis=0).astype(BF16)
    send_ref[...] = dotb(pick, jnp.concatenate([normed[:, :half], normed[:, half:]], axis=0), 0, 0).astype(BF16)
    both = jnp.concatenate([jnp.where(low, weight, 0.0), jnp.where(low, 0.0, weight)], axis=0)
    hi, lo = split(both)
    pick_ref[: 2 * tokens] = hi
    pick_ref[2 * tokens :] = lo


def shared_kernel(norm_ref, gate_ref, sgu_hbm, sdown_hbm, out_ref, sgu_ref, sdown_ref, sem):
    pairs = ((sgu_hbm, sgu_ref), (sdown_hbm, sdown_ref))
    copies = [pltpu.make_async_copy(src, dst, sem.at[i]) for i, (src, dst) in enumerate(pairs)]
    for copy in copies:
        copy.start()
    normed = norm_ref[...]
    score = jnp.sum(normed.astype(F32) * gate_ref[...], axis=1, keepdims=True)
    copies[0].wait()
    act = (silu(dotb(normed, sgu_ref[0])) * dotb(normed, sgu_ref[1])).astype(BF16)
    copies[1].wait()
    out_ref[...] = jax.nn.sigmoid(score) * dotb(act, sdown_ref[...])


def expert_kernel(recv_ref, gu_hbm, down_ref, out_hbm, gu_ref, flat_ref, x_ref, out_ref, gu_sem, sem):
    loads = [pltpu.make_async_copy(gu_hbm.at[e, z], gu_ref.at[e, z], gu_sem.at[2 * e + z]) for e in range(2) for z in range(2)]
    for load in loads:
        load.start()
    rows, half = recv_ref.shape
    srcs = rows // 8
    flat = functools.partial(pl.ds, size=srcs, stride=8)
    lanes = 128
    for c in range(half // lanes):
        at = slice(c * lanes, (c + 1) * lanes)
        flat_ref[c] = recv_ref[:, at].astype(F32)
        for e in range(2):
            for r in range(2):
                for b in range(2):
                    x_ref[e, r * srcs : (r + 1) * srcs, b * half + c * lanes : b * half + (c + 1) * lanes] = flat_ref[
                        c, flat(4 * e + 2 * r + b), :
                    ].astype(BF16)
    acts = []
    for e in range(2):
        x = x_ref[e]
        loads[2 * e].wait()
        gate = silu(dotb(x, gu_ref[e, 0]))
        loads[2 * e + 1].wait()
        acts.append((gate * dotb(x, gu_ref[e, 1])).astype(BF16))
    wide = 2 * lanes
    copies = []
    for p in range(half // wide):
        for e in range(2):
            for b in range(2):
                y = dotb(acts[e], down_ref[e, :, b * half + p * wide : b * half + (p + 1) * wide])
                for r in range(2):
                    for c in range(2):
                        flat_ref[2 * p + c, flat(4 * e + 2 * r + b), :] = y[
                            r * srcs : (r + 1) * srcs, c * lanes : (c + 1) * lanes
                        ]
        for c in (2 * p, 2 * p + 1):
            out_ref[:, c * lanes : (c + 1) * lanes] = flat_ref[c].astype(BF16)
        at = slice(p * wide, (p + 1) * wide)
        copies.append(pltpu.make_async_copy(out_ref.at[:, at], out_hbm.at[:, at], sem.at[p]))
        copies[-1].start()
    for copy in copies:
        copy.wait()


def combine_kernel(back_ref, pick_ref, shared_ref, out_ref):
    got = dotb(pick_ref[...], back_ref[...])
    n = got.shape[0] // 4
    half = got.shape[1]
    got = got[: 2 * n] + got[2 * n :]
    out_ref[:, :half] = (got[:n] + shared_ref[:, :half]).astype(BF16)
    out_ref[:, half:] = (got[n:] + shared_ref[:, half:]).astype(BF16)


def shards(
    qk_proj,
    v_proj,
    z_proj,
    conv_qk,
    conv_v,
    decay_log,
    beta_gate,
    doc_ids,
    head_gain,
    out_weight,
    residual,
    post_gain,
    route_ids,
    route_weight,
    expert_gate_up,
    expert_down,
    shared_gate_up,
    shared_down,
    shared_gate,
):
    seq_n, exp_n = lax.axis_size("seq"), lax.axis_size("exp")
    runs = [[g * RUN + i for i in range(RUN)] for g in range(seq_n // RUN)]
    q, k = qk_proj[:, 0], qk_proj[:, 1]
    rim = jnp.concatenate([q[L - 8 :], k[L - 8 :], v_proj[L - 8 :]], axis=1)
    halo = lax.ppermute(rim, "seq", [(i, i + 1) for i in range(seq_n - 1)])

    wide = 2 * q.shape[1] + v_proj.shape[1]
    conv, edge, within, system, cols = call(
        prep_kernel,
        (
            near((L, wide), F32),
            near((16, wide), F32),
            near((HEADS, L, L), F32),
            near((HEADS, L, L), F32),
            near((L, L), F32),
        ),
        q, k, v_proj, conv_qk, conv_v, decay_log, beta_gate, doc_ids.reshape(seq_n, L),
        hbm=range(8),
        scratch=[
            pltpu.VMEM((L, wide), BF16),
            pltpu.VMEM(conv_qk.shape, F32),
            pltpu.VMEM(conv_v.shape, F32),
            pltpu.VMEM((2, HEADS, L), F32),
            pltpu.VMEM((seq_n, L), jnp.int32),
            pltpu.SemaphoreType.DMA((8,)),
        ],
        flops=10**8,
        name="prep",
    )
    maps, scores, uw, cq = call(
        maps_kernel,
        (
            near((HEADS, 2 * HD, HD), BF16),
            near((HEADS, L, L), F32),
            near((HEADS, L, 2 * HD), F32),
            near((HEADS, L, HD), F32),
        ),
        conv, edge, halo, within, system, cols,
        flops=2 * 10**9,
        name="maps",
    )
    maps = lax.all_to_all(maps, "seq", split_axis=0, concat_axis=0, tiled=True, axis_index_groups=runs)
    local_out, query_eff = call(
        local_kernel,
        (near((HEADS, L, HD), F32), near((HEADS, L, 2 * HD), BF16)),
        scores, uw, cq,
        flops=10**8,
        name="local_out",
    )
    pq, end = call(
        chain_kernel,
        (near((RUN, HD, 2 * HD), F32), near((HD, HD), BF16)),
        maps,
        flops=10**8,
        name="chain",
    )
    end = lax.ppermute(end, "seq", [(i, i + RUN) for i in range(seq_n - RUN)])
    end, local_out, query_eff = lax.optimization_barrier((end, local_out, query_eff))
    starts = call(starts_kernel, (near((RUN, HD, HD), BF16),), pq, end, flops=10**8, name="starts")
    starts = lax.all_to_all(starts, "seq", split_axis=0, concat_axis=0, tiled=True, axis_index_groups=runs)

    model = out_weight.shape[1]
    rows = residual.shape[0]
    piece = near((rows, model), BF16)
    own, *sends = call(
        project_kernel,
        (near((rows, model), F32), piece, piece, piece),
        local_out, query_eff, starts, z_proj, head_gain.reshape(1, HD), out_weight,
        vmem=(3, 5),
        scratch=[pltpu.VMEM((L, model), F32)],
        flops=6 * 10**8,
        name="project",
    )
    got = {}
    for s in (2, 1, 3):
        got[s] = lax.ppermute(sends[s - 1], "exp", [(i, (i + s) % exp_n) for i in range(exp_n)])
    devices = seq_n * exp_n
    slots = devices * 8
    half = model // 2
    hidden_mid, normed, send, pick = call(
        route_kernel,
        (free((rows, model), BF16), piece, near((slots, half), BF16), near((4 * rows, slots), BF16)),
        own, got[1], got[2], got[3], residual, post_gain.reshape(1, model), route_ids, route_weight,
        flops=2 * 10**8,
        name="route",
    )
    axes = ("seq", "exp")
    recv = lax.all_to_all(send.reshape(devices, 8, half), axes, split_axis=0, concat_axis=0, tiled=True)
    made = call(
        expert_kernel,
        (far((slots, half), BF16),),
        recv.reshape(slots, half), expert_gate_up, expert_down,
        hbm=(1,),
        vmem=(2,),
        scratch=[
            pltpu.VMEM(expert_gate_up.shape, BF16),
            pltpu.VMEM((half // 128, slots, 128), F32),
            pltpu.VMEM((2, 2 * devices, model), BF16),
            pltpu.VMEM((slots, half), BF16),
            pltpu.SemaphoreType.DMA((4,)),
            pltpu.SemaphoreType.DMA((half // 256,)),
        ],
        flops=4 * 10**9,
        name="experts",
    )
    made, normed = lax.optimization_barrier((made, normed))
    shared = call(
        shared_kernel,
        (near((rows, model), F32),),
        normed, shared_gate.reshape(1, model), shared_gate_up, shared_down,
        hbm=(2, 3),
        scratch=[
            pltpu.VMEM(shared_gate_up.shape, BF16),
            pltpu.VMEM(shared_down.shape, BF16),
            pltpu.SemaphoreType.DMA((2,)),
        ],
        flops=2 * 10**8,
        name="shared",
    )
    back = lax.all_to_all(made.reshape(devices, 8, half), axes, split_axis=0, concat_axis=0, tiled=True)
    moe_out = call(
        combine_kernel,
        (free((rows, model), BF16),),
        back.reshape(slots, half), pick, shared,
        flops=3 * 10**8,
        name="combine",
    )
    return hidden_mid, moe_out


def solution(mesh):
    placed = (
        P("seq", None, "exp"),
        P("seq", "exp"),
        P("seq", "exp"),
        P(None, None, "exp"),
        P(None, "exp"),
        P("exp", "seq"),
        P("exp", "seq"),
        P(),
        P(),
        P("exp", None),
        P(("seq", "exp"), None),
        P(),
        P(("seq", "exp"), None),
        P(("seq", "exp"), None),
        P(("seq", "exp"), None, None, None),
        P(("seq", "exp"), None, None),
        P(),
        P(),
        P(),
    )
    return jax.shard_map(
        shards,
        mesh=mesh,
        in_specs=placed,
        out_specs=(P(("seq", "exp"), None), P(("seq", "exp"), None)),
        check_vma=False,
    )
```

```python
import functools

import jax
import jax.numpy as jnp
from jax import lax
from jax.experimental import pallas as pl
from jax.experimental.pallas import tpu as pltpu
from jax.sharding import PartitionSpec as P

F32 = jnp.float32
BF16 = jnp.bfloat16
HIGH = lax.Precision.HIGHEST
L = 128
HD = 128
HEADS = 8
RUN = 8
VMEM_CAP = 28 * 1024 * 1024


def dotf(a, b, ca=1, cb=0):
    return lax.dot_general(a, b, (((ca,), (cb,)), ((), ())), precision=HIGH, preferred_element_type=F32)


def dotb(a, b, ca=1, cb=0):
    return lax.dot_general(a, b, (((ca,), (cb,)), ((), ())), preferred_element_type=F32)


def split(x):
    hi = x.astype(BF16)
    return hi, (x - hi.astype(F32)).astype(BF16)


def silu(x):
    return x * jax.nn.sigmoid(x)


def call(body, outs, *args, scratch=(), hbm=(), vmem=(), flops=0, name=None):
    here, far_spec = pl.BlockSpec(memory_space=pltpu.VMEM), pl.BlockSpec(memory_space=pltpu.HBM)
    size = sum(a.size * a.dtype.itemsize for a in args)
    held = {i: pltpu.HBM for i in hbm} | {i: pltpu.VMEM for i in vmem}
    args = [pltpu.with_memory_space_constraint(a, held[i]) if i in held else a for i, a in enumerate(args)]
    made = pl.pallas_call(
        body,
        out_shape=[place(o.shape, o.dtype) if place else o for o, place in outs],
        in_specs=[far_spec if i in hbm else here for i in range(len(args))],
        out_specs=[far_spec if place is pltpu.HBM else here for _, place in outs],
        scratch_shapes=list(scratch),
        compiler_params=pltpu.CompilerParams(vmem_limit_bytes=VMEM_CAP),
        cost_estimate=pl.CostEstimate(flops=flops, bytes_accessed=size, transcendentals=0),
        name=name,
    )(*args)
    return made[0] if len(outs) == 1 else made


def near(shape, dtype):
    return jax.ShapeDtypeStruct(shape, dtype), pltpu.VMEM


def far(shape, dtype):
    return jax.ShapeDtypeStruct(shape, dtype), pltpu.HBM


def free(shape, dtype):
    return jax.ShapeDtypeStruct(shape, dtype), None


def iota(shape, dim):
    return lax.broadcasted_iota(jnp.int32, shape, dim)


def dot3(a, b, ca=1, cb=0):
    ah, al = split(a)
    bh, bl = split(b)
    return dotb(jnp.concatenate([ah, al, ah], axis=ca), jnp.concatenate([bh, bh, bl], axis=cb), ca, cb)


def rim_kernel(qk_hbm, v_hbm, rim_ref, qk_ref, v_ref, sem):
    tail = pl.ds(L - 8, 8)
    copies = [
        pltpu.make_async_copy(qk_hbm.at[tail], qk_ref, sem.at[0]),
        pltpu.make_async_copy(v_hbm.at[tail], v_ref, sem.at[1]),
    ]
    for copy in copies:
        copy.start()
    for copy in copies:
        copy.wait()
    kw = qk_ref.shape[2]
    for z in range(2):
        rim_ref[:, z * kw : (z + 1) * kw] = qk_ref[:, z, :]
    rim_ref[:, 2 * kw :] = v_ref[...]


def prep_kernel(qk_hbm, v_hbm, cqk_hbm, cv_hbm, decay_hbm, beta_hbm, doc_hbm, conv_ref, edge_ref, within_ref, sys_ref, cols_ref, qk_ref, v_ref, cqk_ref, cv_ref, db_ref, doc_ref, sem):
    kw = qk_hbm.shape[2]
    vw = v_hbm.shape[1]
    pairs = (
        (doc_hbm, doc_ref),
        (decay_hbm, db_ref.at[0]),
        (beta_hbm, db_ref.at[1]),
        (cqk_hbm, cqk_ref),
        (cv_hbm, cv_ref),
        (qk_hbm, qk_ref),
        (v_hbm, v_ref),
    )
    copies = [pltpu.make_async_copy(src, dst, sem.at[i]) for i, (src, dst) in enumerate(pairs)]
    for copy in copies:
        copy.start()
    for copy in copies[:3]:
        copy.wait()
    me = lax.axis_index("seq")
    cur = doc_ref[pl.ds(me, 1), :]
    prev = doc_ref[pl.ds(jnp.maximum(me - 1, 0), 1), :]
    prev = jnp.where(me == 0, -1, prev)
    cur8 = jnp.broadcast_to(cur, (8, L)).astype(F32)
    prev8 = jnp.broadcast_to(prev, (8, L)).astype(F32)
    lane8 = iota((8, L), 1)
    row8 = iota((8, L), 0)
    cum = db_ref[0]
    for step in (1, 2, 4, 8, 16, 32, 64):
        cum = cum + jnp.where(lane8 >= step, pltpu.roll(cum, step, 1), 0.0)
    flags = (cur8 == prev8[:, L - 1 :]).astype(F32)
    for s in (1, 2, 3):
        shifted = jnp.where(lane8 < s, pltpu.roll(prev8, s, 1), pltpu.roll(cur8, s, 1))
        flags = jnp.where(row8 == s, (shifted == cur8).astype(F32), flags)
    flags = jnp.where(row8 == 4, cur8, flags)
    last = L - 1
    doc_row = cur8[:1]
    end_same = cur8 == cur8[:, last:]
    carried = jnp.exp(cum) * (cur8 == prev8[:, last:]).astype(F32)
    ends = jnp.where(end_same, jnp.exp(jnp.where(end_same, cum[:, last:] - cum, 0.0)), 0.0)
    rows = jnp.concatenate([cum, db_ref[1], flags, carried, ends, jnp.zeros((L - 40, L), F32)], axis=0)
    cols = rows.T
    cols_ref[...] = cols
    doc_col = cols[:, 20:21]
    ri, ci = iota((L, L), 0), iota((L, L), 1)
    keep = (doc_col == doc_row) & (ri >= ci)
    strict = ri > ci
    for h in range(HEADS):
        spread = cols[:, h : h + 1] - cum[h : h + 1]
        within = jnp.where(keep, jnp.exp(jnp.where(keep, spread, 0.0)), 0.0)
        within_ref[h] = within
        sys_ref[h] = jnp.where(strict, cols[:, 8 + h : 9 + h] * within, 0.0)
    for copy in copies[3:]:
        copy.wait()

    def taps(i, at, half):
        if half is None:
            return cv_ref[i : i + 1, at]
        return cqk_ref[i, half : half + 1, at]

    step = 256
    for start in range(0, 2 * kw + vw, step):
        if start < 2 * kw:
            half, off = start // kw, start % kw
        else:
            half, off = None, start - 2 * kw
        at, here = slice(off, off + step), slice(start, start + step)
        x = (v_ref[:, at] if half is None else qk_ref[:, half, at]).astype(F32)
        row = iota((8, step), 0)
        total = taps(3, at, half) * x
        for s in (1, 2, 3):
            moved = pltpu.roll(x, s, 0)
            moved = jnp.concatenate([jnp.where(row < s, 0.0, moved[:8]), moved[8:]], axis=0)
            total = total + taps(3 - s, at, half) * (moved * cols[:, 16 + s : 17 + s])
            edge_ref[8 + s : 9 + s, here] = taps(3 - s, at, half)
        edge_ref[:8, here] = total[:8]
        conv_ref[:, here] = silu(total)


def maps_kernel(conv_ref, edge_ref, halo_ref, within_ref, sys_ref, cols_ref, maps_ref, sc_ref, uw_ref, cq_ref):
    cols = cols_ref[...]
    halo = halo_ref[...].astype(F32)
    row8 = iota(halo.shape, 0)
    first = edge_ref[:8]
    for s in (1, 2, 3):
        moved = jnp.where(row8 < s, pltpu.roll(halo, s, 0), 0.0)
        first = first + edge_ref[8 + s : 9 + s] * (moved * cols[:8, 16 + s : 17 + s])
    first = silu(first)

    def feature(j):
        at = slice(j * HD, (j + 1) * HD)
        return jnp.concatenate([first[:, at], conv_ref[8:, at]], axis=0)

    ri, ci = iota((L, L), 0), iota((L, L), 1)
    eye = (ri == ci).astype(F32)
    pairs = HEADS // 2
    q_heads, k_heads, kk, qk = [], [], [], []
    for j in range(pairs):
        qj, kj = feature(j), feature(pairs + j)
        qj = qj * lax.rsqrt(jnp.sum(qj * qj, axis=1, keepdims=True) + 1e-06) * (HD ** -0.5)
        kj = kj * lax.rsqrt(jnp.sum(kj * kj, axis=1, keepdims=True) + 1e-06)
        q_heads.append(qj)
        k_heads.append(kj)
        dots = dot3(jnp.concatenate([qj, kj], axis=0), kj, 1, 1)
        qk.append(dots[:L])
        kk.append(dots[L:])
    systems = [sys_ref[h] * kk[h // 2] for h in range(HEADS)]
    narrow = [a.astype(BF16) for a in systems]
    zero = jnp.zeros((L, L), BF16)
    one = ri // 2 == ci // 2
    inverses = [eye - jnp.where(one, a, 0.0) for a in systems]
    size = 2
    while size < L:
        pick = (ri // (2 * size) == ci // (2 * size)) & (ri // size != ci // size)
        low = [x.astype(BF16) for x in inverses]
        inner = [dotb(jnp.where(pick, a, zero), x) for a, x in zip(narrow, low)]
        inverses = [x - dotb(b, y.astype(BF16)) for x, b, y in zip(inverses, low, inner)]
        size *= 2
    rests = [eye - x - dot3(a, x) for a, x in zip(systems, inverses)]
    inverses = [x + dotb(x.astype(BF16), r.astype(BF16)) for x, r in zip(inverses, rests)]
    for h in range(HEADS):
        kj = k_heads[h // 2]
        b_col = cols[:, 8 + h : 9 + h]
        carried = cols[:, 24 + h : 25 + h]
        right = jnp.concatenate([b_col * feature(2 * pairs + h), (b_col * carried) * kj], axis=1)
        uw = dot3(inverses[h], right)
        uw_ref[h] = uw
        sc_ref[h] = qk[h // 2] * within_ref[h]
        cq_ref[h] = carried * q_heads[h // 2]
        ends = dot3(cols[:, 32 + h : 33 + h] * kj, uw, 0, 0)
        maps_ref[h, :L] = (carried[L - 1 :] * eye - ends[:, HD:]).astype(BF16)
        maps_ref[h, L:] = ends[:, :HD].astype(BF16)


def local_kernel(sc_ref, uw_ref, cq_ref, out_ref, qe_ref):
    for h in range(HEADS):
        both = dot3(sc_ref[h], uw_ref[h])
        out_ref[h] = both[:, :HD]
        hi, lo = split(cq_ref[h] - both[:, HD:])
        qe_ref[h, :, :HD] = hi
        qe_ref[h, :, HD:] = lo


def chain_kernel(maps_ref, pq_ref, end_ref):
    ri, ci = iota((HD, HD), 0), iota((HD, HD), 1)
    state = jnp.concatenate([jnp.zeros((HD, HD), F32), (ri == ci).astype(F32)], axis=1)
    for i in range(RUN):
        pq_ref[i] = state
        trans = maps_ref[i, :HD]
        offset = maps_ref[i, HD:].astype(F32)
        if i == 0:
            state = jnp.concatenate([offset, trans.astype(F32)], axis=1)
            continue
        hi, lo = split(state)
        moved = dotb(jnp.concatenate([trans, trans], axis=1), jnp.concatenate([hi, lo], axis=0))
        state = jnp.concatenate([moved[:, :HD] + offset, moved[:, HD:]], axis=1)
    end_ref[...] = state[:, :HD].astype(BF16)


def starts_kernel(pq_ref, end_ref, start_ref):
    end = end_ref[...]
    ends = jnp.concatenate([end, end], axis=0)
    for i in range(RUN):
        hi, lo = split(pq_ref[i, :, HD:])
        moved = dotb(jnp.concatenate([hi, lo], axis=1), ends)
        start_ref[i] = (pq_ref[i, :, :HD] + moved).astype(BF16)


def project_kernel(out_ref, qe_ref, start_ref, z_ref, gain_ref, w_ref, own_ref, s1_ref, s2_ref, s3_ref, part_ref):
    gain = gain_ref[...]
    gated = []
    for h in range(HEADS):
        start = start_ref[h]
        attn = out_ref[h] + dotb(qe_ref[h], jnp.concatenate([start, start], axis=0))
        z = z_ref[:, h * HD : (h + 1) * HD].astype(F32)
        scale = lax.rsqrt(jnp.mean(attn * attn, axis=1, keepdims=True) + 1e-06)
        gated.append((attn * scale * gain * silu(z)).astype(BF16))
    part_ref[...] = dotb(jnp.concatenate(gated, axis=1), w_ref[...])
    me = lax.axis_index("exp")
    n = own_ref.shape[0]
    own_ref[...] = part_ref[pl.ds(pl.multiple_of(me * n, n), n)]
    for s, ref in ((1, s1_ref), (2, s2_ref), (3, s3_ref)):
        to = lax.rem(me + s, 4)
        ref[...] = part_ref[pl.ds(pl.multiple_of(to * n, n), n)].astype(BF16)


def route_kernel(own_ref, r1_ref, r2_ref, r3_ref, res_ref, gain_ref, ids_ref, wt_ref, mid_ref, norm_ref, send_ref, pick_ref):
    hidden = own_ref[...] + r1_ref[...].astype(F32) + r2_ref[...].astype(F32) + r3_ref[...].astype(F32)
    hidden = res_ref[...].astype(F32) + hidden
    mid_ref[...] = hidden.astype(BF16)
    normed = hidden * lax.rsqrt(jnp.mean(hidden * hidden, axis=1, keepdims=True) + 1e-06) * gain_ref[...]
    normed = normed.astype(BF16)
    norm_ref[...] = normed
    tokens, width = normed.shape
    half = width // 2
    slots = send_ref.shape[0]
    col = iota((tokens, slots), 1)
    expert = col // 4
    rank = (col // 2) % 2
    named = jnp.zeros((tokens, slots), F32)
    weight = jnp.zeros((tokens, slots), F32)
    ti, tj = iota((tokens, tokens), 0), iota((tokens, tokens), 1)
    same = (ti == tj).astype(F32)
    ids = dotf(same, ids_ref[...].astype(F32), 1, 1)
    weights = dotf(same, wt_ref[...], 1, 1)
    expert = expert.astype(F32)
    for k in range(ids_ref.shape[0]):
        hit = expert == ids[:, k : k + 1]
        named = jnp.where(hit, 1.0, named)
        weight = jnp.where(hit, weights[:, k : k + 1], weight)
    before = (ti > tj).astype(BF16)
    earlier = dotb(before, named.astype(BF16))
    chosen = jnp.where(earlier == rank.astype(F32), named, 0.0)
    weight = chosen * weight
    low = col % 2 == 0
    pick = jnp.concatenate([jnp.where(low, chosen, 0.0), jnp.where(low, 0.0, chosen)], axis=0).astype(BF16)
    send_ref[...] = dotb(pick, jnp.concatenate([normed[:, :half], normed[:, half:]], axis=0), 0, 0).astype(BF16)
    both = jnp.concatenate([jnp.where(low, weight, 0.0), jnp.where(low, 0.0, weight)], axis=0)
    hi, lo = split(both)
    pick_ref[: 2 * tokens] = hi
    pick_ref[2 * tokens :] = lo


def shared_kernel(norm_ref, gate_ref, sgu_hbm, sdown_hbm, out_ref, sgu_ref, sdown_ref, sem):
    pairs = ((sgu_hbm, sgu_ref), (sdown_hbm, sdown_ref))
    copies = [pltpu.make_async_copy(src, dst, sem.at[i]) for i, (src, dst) in enumerate(pairs)]
    for copy in copies:
        copy.start()
    normed = norm_ref[...]
    score = jnp.sum(normed.astype(F32) * gate_ref[...], axis=1, keepdims=True)
    copies[0].wait()
    act = (silu(dotb(normed, sgu_ref[0])) * dotb(normed, sgu_ref[1])).astype(BF16)
    copies[1].wait()
    out_ref[...] = jax.nn.sigmoid(score) * dotb(act, sdown_ref[...])


def fetch_kernel(gu_hbm, down_hbm, gu_ref, down_ref, sem):
    copies = [
        pltpu.make_async_copy(src.at[e], dst.at[e], sem.at[2 * i + e])
        for i, (src, dst) in enumerate(((gu_hbm, gu_ref), (down_hbm, down_ref)))
        for e in range(2)
    ]
    for copy in copies:
        copy.start()
    for copy in copies:
        copy.wait()


def expert_kernel(recv_ref, gu_ref, down_ref, out_hbm, flat_ref, x_ref, out_ref, sem):
    rows, half = recv_ref.shape
    srcs = rows // 8
    flat = functools.partial(pl.ds, size=srcs, stride=8)
    lanes = 128
    for c in range(half // lanes):
        at = slice(c * lanes, (c + 1) * lanes)
        flat_ref[c] = recv_ref[:, at].astype(F32)
        for e in range(2):
            for r in range(2):
                for b in range(2):
                    x_ref[e, r * srcs : (r + 1) * srcs, b * half + c * lanes : b * half + (c + 1) * lanes] = flat_ref[
                        c, flat(4 * e + 2 * r + b), :
                    ].astype(BF16)
    acts = []
    for e in range(2):
        x = x_ref[e]
        acts.append((silu(dotb(x, gu_ref[e, 0])) * dotb(x, gu_ref[e, 1])).astype(BF16))
    wide = 2 * lanes
    copies = []
    for p in range(half // wide):
        for e in range(2):
            for b in range(2):
                y = dotb(acts[e], down_ref[e, :, b * half + p * wide : b * half + (p + 1) * wide])
                for r in range(2):
                    for c in range(2):
                        flat_ref[2 * p + c, flat(4 * e + 2 * r + b), :] = y[
                            r * srcs : (r + 1) * srcs, c * lanes : (c + 1) * lanes
                        ]
        for c in (2 * p, 2 * p + 1):
            out_ref[:, c * lanes : (c + 1) * lanes] = flat_ref[c].astype(BF16)
        at = slice(p * wide, (p + 1) * wide)
        copies.append(pltpu.make_async_copy(out_ref.at[:, at], out_hbm.at[:, at], sem.at[p]))
        copies[-1].start()
    for copy in copies:
        copy.wait()


def combine_kernel(back_ref, pick_ref, shared_ref, out_ref):
    got = dotb(pick_ref[...], back_ref[...])
    n = got.shape[0] // 4
    half = got.shape[1]
    got = got[: 2 * n] + got[2 * n :]
    out_ref[:, :half] = (got[:n] + shared_ref[:, :half]).astype(BF16)
    out_ref[:, half:] = (got[n:] + shared_ref[:, half:]).astype(BF16)


def shards(
    qk_proj,
    v_proj,
    z_proj,
    conv_qk,
    conv_v,
    decay_log,
    beta_gate,
    doc_ids,
    head_gain,
    out_weight,
    residual,
    post_gain,
    route_ids,
    route_weight,
    expert_gate_up,
    expert_down,
    shared_gate_up,
    shared_down,
    shared_gate,
):
    seq_n, exp_n = lax.axis_size("seq"), lax.axis_size("exp")
    runs = [[g * RUN + i for i in range(RUN)] for g in range(seq_n // RUN)]
    kw, vw = qk_proj.shape[2], v_proj.shape[1]
    wide = 2 * kw + vw
    rim = call(
        rim_kernel,
        (near((8, wide), BF16),),
        qk_proj, v_proj,
        hbm=(0, 1),
        scratch=[pltpu.VMEM((8, 2, kw), BF16), pltpu.VMEM((8, vw), BF16), pltpu.SemaphoreType.DMA((2,))],
        name="rim",
    )
    halo = lax.ppermute(rim, "seq", [(i, i + 1) for i in range(seq_n - 1)])

    conv, edge, within, system, cols = call(
        prep_kernel,
        (
            near((L, wide), F32),
            near((16, wide), F32),
            near((HEADS, L, L), F32),
            near((HEADS, L, L), F32),
            near((L, L), F32),
        ),
        qk_proj, v_proj, conv_qk, conv_v, decay_log, beta_gate, doc_ids.reshape(seq_n, L),
        hbm=range(7),
        scratch=[
            pltpu.VMEM((L, 2, kw), BF16),
            pltpu.VMEM((L, vw), BF16),
            pltpu.VMEM(conv_qk.shape, F32),
            pltpu.VMEM(conv_v.shape, F32),
            pltpu.VMEM((2, HEADS, L), F32),
            pltpu.VMEM((seq_n, L), jnp.int32),
            pltpu.SemaphoreType.DMA((7,)),
        ],
        flops=10**8,
        name="prep",
    )
    maps, scores, uw, cq = call(
        maps_kernel,
        (
            near((HEADS, 2 * HD, HD), BF16),
            near((HEADS, L, L), F32),
            near((HEADS, L, 2 * HD), F32),
            near((HEADS, L, HD), F32),
        ),
        conv, edge, halo, within, system, cols,
        flops=2 * 10**9,
        name="maps",
    )
    maps = lax.all_to_all(maps, "seq", split_axis=0, concat_axis=0, tiled=True, axis_index_groups=runs)
    local_out, query_eff = call(
        local_kernel,
        (near((HEADS, L, HD), F32), near((HEADS, L, 2 * HD), BF16)),
        scores, uw, cq,
        flops=10**8,
        name="local_out",
    )
    pq, end = call(
        chain_kernel,
        (near((RUN, HD, 2 * HD), F32), near((HD, HD), BF16)),
        maps,
        flops=10**8,
        name="chain",
    )
    end = lax.ppermute(end, "seq", [(i, i + RUN) for i in range(seq_n - RUN)])
    end, local_out, query_eff = lax.optimization_barrier((end, local_out, query_eff))
    starts = call(starts_kernel, (near((RUN, HD, HD), BF16),), pq, end, flops=10**8, name="starts")
    starts = lax.all_to_all(starts, "seq", split_axis=0, concat_axis=0, tiled=True, axis_index_groups=runs)

    model = out_weight.shape[1]
    rows = residual.shape[0]
    piece = near((rows, model), BF16)
    own, *sends = call(
        project_kernel,
        (near((rows, model), F32), piece, piece, piece),
        local_out, query_eff, starts, z_proj, head_gain.reshape(1, HD), out_weight,
        vmem=(3, 5),
        scratch=[pltpu.VMEM((L, model), F32)],
        flops=6 * 10**8,
        name="project",
    )
    got = {}
    for s in (2, 1, 3):
        got[s] = lax.ppermute(sends[s - 1], "exp", [(i, (i + s) % exp_n) for i in range(exp_n)])
    gu_near, down_near = call(
        fetch_kernel,
        (near(expert_gate_up.shape, BF16), near(expert_down.shape, BF16)),
        expert_gate_up, expert_down,
        hbm=(0, 1),
        scratch=[pltpu.SemaphoreType.DMA((4,))],
        name="fetch",
    )
    own, gu_near, down_near = lax.optimization_barrier((own, gu_near, down_near))
    devices = seq_n * exp_n
    slots = devices * 8
    half = model // 2
    hidden_mid, normed, send, pick = call(
        route_kernel,
        (free((rows, model), BF16), piece, near((slots, half), BF16), near((4 * rows, slots), BF16)),
        own, got[1], got[2], got[3], residual, post_gain.reshape(1, model), route_ids.T, route_weight.T,
        flops=2 * 10**8,
        name="route",
    )
    axes = ("seq", "exp")
    recv = lax.all_to_all(send.reshape(devices, 8, half), axes, split_axis=0, concat_axis=0, tiled=True)
    made = call(
        expert_kernel,
        (far((slots, half), BF16),),
        recv.reshape(slots, half), gu_near, down_near,
        scratch=[
            pltpu.VMEM((half // 128, slots, 128), F32),
            pltpu.VMEM((2, 2 * devices, model), BF16),
            pltpu.VMEM((slots, half), BF16),
            pltpu.SemaphoreType.DMA((half // 256,)),
        ],
        flops=4 * 10**9,
        name="experts",
    )
    made, normed = lax.optimization_barrier((made, normed))
    shared = call(
        shared_kernel,
        (near((rows, model), F32),),
        normed, shared_gate.reshape(1, model), shared_gate_up, shared_down,
        hbm=(2, 3),
        scratch=[
            pltpu.VMEM(shared_gate_up.shape, BF16),
            pltpu.VMEM(shared_down.shape, BF16),
            pltpu.SemaphoreType.DMA((2,)),
        ],
        flops=2 * 10**8,
        name="shared",
    )
    back = lax.all_to_all(made.reshape(devices, 8, half), axes, split_axis=0, concat_axis=0, tiled=True)
    moe_out = call(
        combine_kernel,
        (free((rows, model), BF16),),
        back.reshape(slots, half), pick, shared,
        flops=3 * 10**8,
        name="combine",
    )
    return hidden_mid, moe_out


def solution(mesh):
    placed = (
        P("seq", None, "exp"),
        P("seq", "exp"),
        P("seq", "exp"),
        P(None, None, "exp"),
        P(None, "exp"),
        P("exp", "seq"),
        P("exp", "seq"),
        P(),
        P(),
        P("exp", None),
        P(("seq", "exp"), None),
        P(),
        P(("seq", "exp"), None),
        P(("seq", "exp"), None),
        P(("seq", "exp"), None, None, None),
        P(("seq", "exp"), None, None),
        P(),
        P(),
        P(),
    )
    return jax.shard_map(
        shards,
        mesh=mesh,
        in_specs=placed,
        out_specs=(P(("seq", "exp"), None), P(("seq", "exp"), None)),
        check_vma=False,
    )
```

```python
import functools

import jax
import jax.numpy as jnp
import numpy as np
from jax import lax
from jax.experimental import pallas as pl
from jax.experimental.pallas import tpu as pltpu
from jax.sharding import PartitionSpec as P

F32 = jnp.float32
BF16 = jnp.bfloat16
HIGH = lax.Precision.HIGHEST
L = 128
HD = 128
HEADS = 8
RUN = 8
VMEM_CAP = 28 * 1024 * 1024


def dotf(a, b, ca=1, cb=0):
    return lax.dot_general(a, b, (((ca,), (cb,)), ((), ())), precision=HIGH, preferred_element_type=F32)


def dotb(a, b, ca=1, cb=0):
    return lax.dot_general(a, b, (((ca,), (cb,)), ((), ())), preferred_element_type=F32)


def split(x):
    hi = x.astype(BF16)
    return hi, (x - hi.astype(F32)).astype(BF16)


def silu(x):
    return x * jax.nn.sigmoid(x)


def call(body, outs, *args, scratch=(), hbm=(), vmem=(), flops=0, name=None):
    here, far_spec = pl.BlockSpec(memory_space=pltpu.VMEM), pl.BlockSpec(memory_space=pltpu.HBM)
    size = sum(a.size * a.dtype.itemsize for a in args)
    held = {i: pltpu.HBM for i in hbm} | {i: pltpu.VMEM for i in vmem}
    args = [pltpu.with_memory_space_constraint(a, held[i]) if i in held else a for i, a in enumerate(args)]
    made = pl.pallas_call(
        body,
        out_shape=[place(o.shape, o.dtype) if place else o for o, place in outs],
        in_specs=[far_spec if i in hbm else here for i in range(len(args))],
        out_specs=[far_spec if place is pltpu.HBM else here for _, place in outs],
        scratch_shapes=list(scratch),
        compiler_params=pltpu.CompilerParams(vmem_limit_bytes=VMEM_CAP),
        cost_estimate=pl.CostEstimate(flops=flops, bytes_accessed=size, transcendentals=0),
        name=name,
    )(*args)
    return made[0] if len(outs) == 1 else made


def near(shape, dtype):
    return jax.ShapeDtypeStruct(shape, dtype), pltpu.VMEM


def far(shape, dtype):
    return jax.ShapeDtypeStruct(shape, dtype), pltpu.HBM


def free(shape, dtype):
    return jax.ShapeDtypeStruct(shape, dtype), None


def iota(shape, dim):
    return lax.broadcasted_iota(jnp.int32, shape, dim)


def dot3(a, b, ca=1, cb=0):
    ah, al = split(a)
    bh, bl = split(b)
    return dotb(jnp.concatenate([ah, al, ah], axis=ca), jnp.concatenate([bh, bh, bl], axis=cb), ca, cb)


def rim_kernel(*refs):
    n = (len(refs) - 2) // 2
    sources, rim_ref, near_refs, sem = refs[:n], refs[n], refs[n + 1 : -1], refs[-1]
    copies = [pltpu.make_async_copy(src, dst, sem.at[i]) for i, (src, dst) in enumerate(zip(sources, near_refs))]
    for copy in copies:
        copy.start()
    copies[0].wait()
    copies[1].wait()
    qk_ref, v_ref = near_refs[:2]
    kw = qk_ref.shape[2]
    for z in range(2):
        rim_ref[:, z * kw : (z + 1) * kw] = qk_ref[L - 8 :, z, :]
    rim_ref[:, 2 * kw :] = v_ref[L - 8 :]
    for copy in copies[2:]:
        copy.wait()


def prep_kernel(qk_ref, v_ref, cqk_ref, cv_ref, decay_ref, beta_ref, doc_ref, conv_ref, edge_ref, within_ref, sys_ref, cols_ref):
    kw = qk_ref.shape[2]
    vw = v_ref.shape[1]
    me = lax.axis_index("seq")
    cur = doc_ref[pl.ds(me, 1), :]
    prev = doc_ref[pl.ds(jnp.maximum(me - 1, 0), 1), :]
    prev = jnp.where(me == 0, -1, prev)
    cur8 = jnp.broadcast_to(cur, (8, L)).astype(F32)
    prev8 = jnp.broadcast_to(prev, (8, L)).astype(F32)
    lane8 = iota((8, L), 1)
    row8 = iota((8, L), 0)
    cum = decay_ref[...]
    for step in (1, 2, 4, 8, 16, 32, 64):
        cum = cum + jnp.where(lane8 >= step, pltpu.roll(cum, step, 1), 0.0)
    flags = (cur8 == prev8[:, L - 1 :]).astype(F32)
    for s in (1, 2, 3):
        shifted = jnp.where(lane8 < s, pltpu.roll(prev8, s, 1), pltpu.roll(cur8, s, 1))
        flags = jnp.where(row8 == s, (shifted == cur8).astype(F32), flags)
    flags = jnp.where(row8 == 4, cur8, flags)
    last = L - 1
    doc_row = cur8[:1]
    end_same = cur8 == cur8[:, last:]
    carried = jnp.exp(cum) * (cur8 == prev8[:, last:]).astype(F32)
    ends = jnp.where(end_same, jnp.exp(jnp.where(end_same, cum[:, last:] - cum, 0.0)), 0.0)
    rows = jnp.concatenate([cum, beta_ref[...], flags, carried, ends, jnp.zeros((L - 40, L), F32)], axis=0)
    cols = rows.T
    cols_ref[...] = cols
    doc_col = cols[:, 20:21]
    ri, ci = iota((L, L), 0), iota((L, L), 1)
    keep = (doc_col == doc_row) & (ri >= ci)
    strict = ri > ci
    for h in range(HEADS):
        spread = cols[:, h : h + 1] - cum[h : h + 1]
        within = jnp.where(keep, jnp.exp(jnp.where(keep, spread, 0.0)), 0.0)
        within_ref[h] = within
        sys_ref[h] = jnp.where(strict, cols[:, 8 + h : 9 + h] * within, 0.0)

    def taps(i, at, half):
        if half is None:
            return cv_ref[i : i + 1, at]
        return cqk_ref[i, half : half + 1, at]

    step = 256
    for start in range(0, 2 * kw + vw, step):
        if start < 2 * kw:
            half, off = start // kw, start % kw
        else:
            half, off = None, start - 2 * kw
        at, here = slice(off, off + step), slice(start, start + step)
        x = (v_ref[:, at] if half is None else qk_ref[:, half, at]).astype(F32)
        row = iota((8, step), 0)
        total = taps(3, at, half) * x
        for s in (1, 2, 3):
            moved = pltpu.roll(x, s, 0)
            moved = jnp.concatenate([jnp.where(row < s, 0.0, moved[:8]), moved[8:]], axis=0)
            total = total + taps(3 - s, at, half) * (moved * cols[:, 16 + s : 17 + s])
            edge_ref[8 + s : 9 + s, here] = taps(3 - s, at, half)
        edge_ref[:8, here] = total[:8]
        conv_ref[:, here] = silu(total)


def maps_kernel(conv_ref, edge_ref, halo_ref, within_ref, sys_ref, cols_ref, maps_ref, sc_ref, uw_ref, cq_ref):
    cols = cols_ref[...]
    halo = halo_ref[...].astype(F32)
    row8 = iota(halo.shape, 0)
    first = edge_ref[:8]
    for s in (1, 2, 3):
        moved = jnp.where(row8 < s, pltpu.roll(halo, s, 0), 0.0)
        first = first + edge_ref[8 + s : 9 + s] * (moved * cols[:8, 16 + s : 17 + s])
    first = silu(first)

    def feature(j):
        at = slice(j * HD, (j + 1) * HD)
        return jnp.concatenate([first[:, at], conv_ref[8:, at]], axis=0)

    ri, ci = iota((L, L), 0), iota((L, L), 1)
    eye = (ri == ci).astype(F32)
    pairs = HEADS // 2
    q_heads, k_heads, kk, qk = [], [], [], []
    for j in range(pairs):
        qj, kj = feature(j), feature(pairs + j)
        qj = qj * lax.rsqrt(jnp.sum(qj * qj, axis=1, keepdims=True) + 1e-06) * (HD ** -0.5)
        kj = kj * lax.rsqrt(jnp.sum(kj * kj, axis=1, keepdims=True) + 1e-06)
        q_heads.append(qj)
        k_heads.append(kj)
        dots = dot3(jnp.concatenate([qj, kj], axis=0), kj, 1, 1)
        qk.append(dots[:L])
        kk.append(dots[L:])
    systems = [sys_ref[h] * kk[h // 2] for h in range(HEADS)]
    narrow = [a.astype(BF16) for a in systems]
    zero = jnp.zeros((L, L), BF16)
    one = ri // 2 == ci // 2
    inverses = [eye - jnp.where(one, a, 0.0) for a in systems]
    size = 2
    while size < L:
        pick = (ri // (2 * size) == ci // (2 * size)) & (ri // size != ci // size)
        low = [x.astype(BF16) for x in inverses]
        inner = [dotb(jnp.where(pick, a, zero), x) for a, x in zip(narrow, low)]
        inverses = [x - dotb(b, y.astype(BF16)) for x, b, y in zip(inverses, low, inner)]
        size *= 2
    rests = [eye - x - dot3(a, x) for a, x in zip(systems, inverses)]
    inverses = [x + dotb(x.astype(BF16), r.astype(BF16)) for x, r in zip(inverses, rests)]
    for h in range(HEADS):
        kj = k_heads[h // 2]
        b_col = cols[:, 8 + h : 9 + h]
        carried = cols[:, 24 + h : 25 + h]
        right = jnp.concatenate([b_col * feature(2 * pairs + h), (b_col * carried) * kj], axis=1)
        uw = dot3(inverses[h], right)
        uw_ref[h] = uw
        sc_ref[h] = qk[h // 2] * within_ref[h]
        cq_ref[h] = carried * q_heads[h // 2]
        ends = dot3(cols[:, 32 + h : 33 + h] * kj, uw, 0, 0)
        maps_ref[h, :L] = (carried[L - 1 :] * eye - ends[:, HD:]).astype(BF16)
        maps_ref[h, L:] = ends[:, :HD].astype(BF16)


def local_kernel(sc_ref, uw_ref, cq_ref, out_ref, qe_ref):
    for h in range(HEADS):
        both = dot3(sc_ref[h], uw_ref[h])
        out_ref[h] = both[:, :HD]
        hi, lo = split(cq_ref[h] - both[:, HD:])
        qe_ref[h, :, :HD] = hi
        qe_ref[h, :, HD:] = lo


def chain_kernel(maps_ref, pq_ref, end_ref):
    ri, ci = iota((HD, HD), 0), iota((HD, HD), 1)
    state = jnp.concatenate([jnp.zeros((HD, HD), F32), (ri == ci).astype(F32)], axis=1)
    for i in range(RUN):
        pq_ref[i] = state
        trans = maps_ref[i, :HD]
        offset = maps_ref[i, HD:].astype(F32)
        if i == 0:
            state = jnp.concatenate([offset, trans.astype(F32)], axis=1)
            continue
        hi, lo = split(state)
        moved = dotb(jnp.concatenate([trans, trans], axis=1), jnp.concatenate([hi, lo], axis=0))
        state = jnp.concatenate([moved[:, :HD] + offset, moved[:, HD:]], axis=1)
    end_ref[...] = state[:, :HD].astype(BF16)


def starts_kernel(pq_ref, end_ref, start_ref):
    end = end_ref[...]
    ends = jnp.concatenate([end, end], axis=0)
    for i in range(RUN):
        hi, lo = split(pq_ref[i, :, HD:])
        moved = dotb(jnp.concatenate([hi, lo], axis=1), ends)
        start_ref[i] = (pq_ref[i, :, :HD] + moved).astype(BF16)


def project_kernel(out_ref, qe_ref, start_ref, z_ref, gain_ref, w_ref, own_ref, s1_ref, s2_ref, s3_ref, part_ref):
    gain = gain_ref[...]
    gated = []
    for h in range(HEADS):
        start = start_ref[h]
        attn = out_ref[h] + dotb(qe_ref[h], jnp.concatenate([start, start], axis=0))
        z = z_ref[:, h * HD : (h + 1) * HD].astype(F32)
        scale = lax.rsqrt(jnp.mean(attn * attn, axis=1, keepdims=True) + 1e-06)
        gated.append((attn * scale * gain * silu(z)).astype(BF16))
    part_ref[...] = dotb(jnp.concatenate(gated, axis=1), w_ref[...])
    me = lax.axis_index("exp")
    n = own_ref.shape[0]
    own_ref[...] = part_ref[pl.ds(pl.multiple_of(me * n, n), n)]
    for s, ref in ((1, s1_ref), (2, s2_ref), (3, s3_ref)):
        to = lax.rem(me + s, 4)
        ref[...] = part_ref[pl.ds(pl.multiple_of(to * n, n), n)].astype(BF16)


def route_kernel(own_ref, r1_ref, r2_ref, r3_ref, res_ref, gain_ref, ids_ref, wt_ref, to_ref, mid_ref, norm_ref, send_ref, pick_ref):
    hidden = own_ref[...] + r1_ref[...].astype(F32) + r2_ref[...].astype(F32) + r3_ref[...].astype(F32)
    hidden = res_ref[...].astype(F32) + hidden
    mid_ref[...] = hidden.astype(BF16)
    normed = hidden * lax.rsqrt(jnp.mean(hidden * hidden, axis=1, keepdims=True) + 1e-06) * gain_ref[...]
    normed = normed.astype(BF16)
    norm_ref[...] = normed
    tokens, width = normed.shape
    half = width // 2
    slots = send_ref.shape[0]
    col = iota((tokens, slots), 1)
    rank = (col // 2) % 2
    named = jnp.zeros((tokens, slots), F32)
    weight = jnp.zeros((tokens, slots), F32)
    ti, tj = iota((tokens, tokens), 0), iota((tokens, tokens), 1)
    same = (ti == tj).astype(F32)
    ids = dotf(same, ids_ref[...].astype(F32), 1, 1)
    weights = dotf(same, wt_ref[...], 1, 1)
    expert = to_ref[...].astype(F32)
    for k in range(ids_ref.shape[0]):
        hit = expert == ids[:, k : k + 1]
        named = jnp.where(hit, 1.0, named)
        weight = jnp.where(hit, weights[:, k : k + 1], weight)
    before = (ti > tj).astype(BF16)
    earlier = dotb(before, named.astype(BF16))
    chosen = jnp.where(earlier == rank.astype(F32), named, 0.0)
    weight = chosen * weight
    low = col % 2 == 0
    pick = jnp.concatenate([jnp.where(low, chosen, 0.0), jnp.where(low, 0.0, chosen)], axis=0).astype(BF16)
    send_ref[...] = dotb(pick, jnp.concatenate([normed[:, :half], normed[:, half:]], axis=0), 0, 0).astype(BF16)
    both = jnp.concatenate([jnp.where(low, weight, 0.0), jnp.where(low, 0.0, weight)], axis=0)
    hi, lo = split(both)
    pick_ref[: 2 * tokens] = hi
    pick_ref[2 * tokens :] = lo


def shared_kernel(norm_ref, gate_ref, sgu_hbm, sdown_hbm, out_ref, sgu_ref, sdown_ref, sem):
    pairs = ((sgu_hbm, sgu_ref), (sdown_hbm, sdown_ref))
    copies = [pltpu.make_async_copy(src, dst, sem.at[i]) for i, (src, dst) in enumerate(pairs)]
    for copy in copies:
        copy.start()
    normed = norm_ref[...]
    score = jnp.sum(normed.astype(F32) * gate_ref[...], axis=1, keepdims=True)
    copies[0].wait()
    act = (silu(dotb(normed, sgu_ref[0])) * dotb(normed, sgu_ref[1])).astype(BF16)
    copies[1].wait()
    out_ref[...] = jax.nn.sigmoid(score) * dotb(act, sdown_ref[...])


def fetch_kernel(gu_hbm, down_hbm, gu_ref, down_ref, sem):
    copies = [
        pltpu.make_async_copy(src.at[e], dst.at[e], sem.at[2 * i + e])
        for i, (src, dst) in enumerate(((gu_hbm, gu_ref), (down_hbm, down_ref)))
        for e in range(2)
    ]
    for copy in copies:
        copy.start()
    for copy in copies:
        copy.wait()


def expert_kernel(recv_ref, gu_ref, down_ref, out_hbm, flat_ref, made_ref, x0_ref, x1_ref, out_ref, sem):
    rows, half = recv_ref.shape
    srcs = rows // 8
    flat = functools.partial(pl.ds, size=srcs, stride=8)
    lanes, wide = 128, 256
    x_refs = (x0_ref, x1_ref)

    def gather(e, c):
        for r in range(2):
            for b in range(2):
                to = slice(b * half + c * lanes, b * half + (c + 1) * lanes)
                x_refs[e][r * srcs : (r + 1) * srcs, to] = flat_ref[c, flat(4 * e + 2 * r + b), :].astype(BF16)

    def down(e, act, p):
        for b in range(2):
            y = dotb(act, down_ref[e, :, b * half + p * wide : b * half + (p + 1) * wide])
            for r in range(2):
                for c in range(2):
                    made_ref[2 * p + c, flat(4 * e + 2 * r + b), :] = y[r * srcs : (r + 1) * srcs, c * lanes : (c + 1) * lanes]

    def hidden(e, n):
        at = slice(n * wide, (n + 1) * wide)
        x = x_refs[e][...]
        return (silu(dotb(x, gu_ref[e, 0, :, at])) * dotb(x, gu_ref[e, 1, :, at])).astype(BF16)

    for c in range(half // lanes):
        flat_ref[c] = recv_ref[:, c * lanes : (c + 1) * lanes].astype(F32)
        gather(0, c)
    parts = gu_ref.shape[3] // wide
    per = half // lanes // parts
    acts = []
    for n in range(parts):
        acts.append(hidden(0, n))
        for c in range(n * per, (n + 1) * per):
            gather(1, c)
    first = jnp.concatenate(acts, axis=1)
    acts = []
    share = half // wide // parts
    for n in range(parts):
        acts.append(hidden(1, n))
        for p in range(n * share, (n + 1) * share):
            down(0, first, p)
    second = jnp.concatenate(acts, axis=1)
    copies = []
    for p in range(half // wide):
        down(1, second, p)
        for c in (2 * p, 2 * p + 1):
            out_ref[:, c * lanes : (c + 1) * lanes] = made_ref[c].astype(BF16)
        at = slice(p * wide, (p + 1) * wide)
        copies.append(pltpu.make_async_copy(out_ref.at[:, at], out_hbm.at[:, at], sem.at[p]))
        copies[-1].start()
    for copy in copies:
        copy.wait()


def combine_kernel(back_ref, pick_ref, shared_ref, out_ref):
    got = dotb(pick_ref[...], back_ref[...])
    n = got.shape[0] // 4
    half = got.shape[1]
    got = got[: 2 * n] + got[2 * n :]
    out_ref[:, :half] = (got[:n] + shared_ref[:, :half]).astype(BF16)
    out_ref[:, half:] = (got[n:] + shared_ref[:, half:]).astype(BF16)


def exchange_order(seq_n, exp_n):
    return [s * exp_n + e for c in range(2) for s in range(c, seq_n, 2) for e in range(exp_n)]


def shards(
    qk_proj,
    v_proj,
    z_proj,
    conv_qk,
    conv_v,
    decay_log,
    beta_gate,
    doc_ids,
    head_gain,
    out_weight,
    residual,
    post_gain,
    route_ids,
    route_weight,
    expert_gate_up,
    expert_down,
    shared_gate_up,
    shared_down,
    shared_gate,
):
    seq_n, exp_n = lax.axis_size("seq"), lax.axis_size("exp")
    runs = [[g * RUN + i for i in range(RUN)] for g in range(seq_n // RUN)]
    kw, vw = qk_proj.shape[2], v_proj.shape[1]
    wide = 2 * kw + vw
    raw = (qk_proj, v_proj, conv_qk, conv_v, decay_log, beta_gate, doc_ids.reshape(seq_n, L))
    rim, *held = call(
        rim_kernel,
        (near((8, wide), BF16), *(near(a.shape, a.dtype) for a in raw)),
        *raw,
        hbm=range(len(raw)),
        scratch=[pltpu.SemaphoreType.DMA((len(raw),))],
        name="rim",
    )
    halo = lax.ppermute(rim, "seq", [(i, i + 1) for i in range(seq_n - 1)])

    conv, edge, within, system, cols = call(
        prep_kernel,
        (
            near((L, wide), F32),
            near((16, wide), F32),
            near((HEADS, L, L), F32),
            near((HEADS, L, L), F32),
            near((L, L), F32),
        ),
        *held,
        flops=10**8,
        name="prep",
    )
    maps, scores, uw, cq = call(
        maps_kernel,
        (
            near((HEADS, 2 * HD, HD), BF16),
            near((HEADS, L, L), F32),
            near((HEADS, L, 2 * HD), F32),
            near((HEADS, L, HD), F32),
        ),
        conv, edge, halo, within, system, cols,
        flops=2 * 10**9,
        name="maps",
    )
    maps = lax.all_to_all(maps, "seq", split_axis=0, concat_axis=0, tiled=True, axis_index_groups=runs)
    local_out, query_eff = call(
        local_kernel,
        (near((HEADS, L, HD), F32), near((HEADS, L, 2 * HD), BF16)),
        scores, uw, cq,
        flops=10**8,
        name="local_out",
    )
    pq, end = call(
        chain_kernel,
        (near((RUN, HD, 2 * HD), F32), near((HD, HD), BF16)),
        maps,
        flops=10**8,
        name="chain",
    )
    end = lax.ppermute(end, "seq", [(i, i + RUN) for i in range(seq_n - RUN)])
    end, local_out, query_eff = lax.optimization_barrier((end, local_out, query_eff))
    starts = call(starts_kernel, (near((RUN, HD, HD), BF16),), pq, end, flops=10**8, name="starts")
    starts = lax.all_to_all(starts, "seq", split_axis=0, concat_axis=0, tiled=True, axis_index_groups=runs)

    model = out_weight.shape[1]
    rows = residual.shape[0]
    piece = near((rows, model), BF16)
    own, *sends = call(
        project_kernel,
        (near((rows, model), F32), piece, piece, piece),
        local_out, query_eff, starts, z_proj, head_gain.reshape(1, HD), out_weight,
        vmem=(3, 5),
        scratch=[pltpu.VMEM((L, model), F32)],
        flops=6 * 10**8,
        name="project",
    )
    got = {}
    for s in (2, 1, 3):
        got[s] = lax.ppermute(sends[s - 1], "exp", [(i, (i + s) % exp_n) for i in range(exp_n)])
    gu_near, down_near = call(
        fetch_kernel,
        (near(expert_gate_up.shape, BF16), near(expert_down.shape, BF16)),
        expert_gate_up, expert_down,
        hbm=(0, 1),
        scratch=[pltpu.SemaphoreType.DMA((4,))],
        name="fetch",
    )
    own, gu_near, down_near = lax.optimization_barrier((own, gu_near, down_near))
    devices = seq_n * exp_n
    slots = devices * 8
    half = model // 2
    order = exchange_order(seq_n, exp_n)
    experts_at = np.repeat(2 * np.asarray(order, np.int32), 8).reshape(1, slots)
    experts_at = experts_at + (np.arange(slots, dtype=np.int32) // 4 % 2)
    hidden_mid, normed, send, pick = call(
        route_kernel,
        (free((rows, model), BF16), piece, near((slots, half), BF16), near((4 * rows, slots), BF16)),
        own, got[1], got[2], got[3], residual, post_gain.reshape(1, model), route_ids.T, route_weight.T, jnp.asarray(experts_at),
        flops=2 * 10**8,
        name="route",
    )
    axes = ("seq", "exp")
    recv = lax.all_to_all(send.reshape(devices, 8, half), axes, split_axis=0, concat_axis=0, tiled=True, axis_index_groups=[order])
    made = call(
        expert_kernel,
        (far((slots, half), BF16),),
        recv.reshape(slots, half), gu_near, down_near,
        scratch=[
            pltpu.VMEM((half // 128, slots, 128), F32),
            pltpu.VMEM((half // 128, slots, 128), F32),
            pltpu.VMEM((2 * devices, model), BF16),
            pltpu.VMEM((2 * devices, model), BF16),
            pltpu.VMEM((slots, half), BF16),
            pltpu.SemaphoreType.DMA((half // 256,)),
        ],
        flops=4 * 10**9,
        name="experts",
    )
    made, normed = lax.optimization_barrier((made, normed))
    shared = call(
        shared_kernel,
        (near((rows, model), F32),),
        normed, shared_gate.reshape(1, model), shared_gate_up, shared_down,
        hbm=(2, 3),
        scratch=[
            pltpu.VMEM(shared_gate_up.shape, BF16),
            pltpu.VMEM(shared_down.shape, BF16),
            pltpu.SemaphoreType.DMA((2,)),
        ],
        flops=2 * 10**8,
        name="shared",
    )
    back = lax.all_to_all(made.reshape(devices, 8, half), axes, split_axis=0, concat_axis=0, tiled=True, axis_index_groups=[order])
    moe_out = call(
        combine_kernel,
        (free((rows, model), BF16),),
        back.reshape(slots, half), pick, shared,
        flops=3 * 10**8,
        name="combine",
    )
    return hidden_mid, moe_out


def solution(mesh):
    placed = (
        P("seq", None, "exp"),
        P("seq", "exp"),
        P("seq", "exp"),
        P(None, None, "exp"),
        P(None, "exp"),
        P("exp", "seq"),
        P("exp", "seq"),
        P(),
        P(),
        P("exp", None),
        P(("seq", "exp"), None),
        P(),
        P(("seq", "exp"), None),
        P(("seq", "exp"), None),
        P(("seq", "exp"), None, None, None),
        P(("seq", "exp"), None, None),
        P(),
        P(),
        P(),
    )
    return jax.shard_map(
        shards,
        mesh=mesh,
        in_specs=placed,
        out_specs=(P(("seq", "exp"), None), P(("seq", "exp"), None)),
        check_vma=False,
    )
```

```python
import functools

import jax
import jax.numpy as jnp
import numpy as np
from jax import lax
from jax.experimental import pallas as pl
from jax.experimental.pallas import tpu as pltpu
from jax.sharding import PartitionSpec as P

F32 = jnp.float32
BF16 = jnp.bfloat16
HIGH = lax.Precision.HIGHEST
L = 128
HD = 128
HEADS = 8
RUN = 8
RUN_ORDER = (0, 2, 4, 6, 1, 3, 5, 7)
VMEM_CAP = 28 * 1024 * 1024


def dotf(a, b, ca=1, cb=0):
    return lax.dot_general(a, b, (((ca,), (cb,)), ((), ())), precision=HIGH, preferred_element_type=F32)


def dotb(a, b, ca=1, cb=0):
    return lax.dot_general(a, b, (((ca,), (cb,)), ((), ())), preferred_element_type=F32)


def split(x):
    hi = x.astype(BF16)
    return hi, (x - hi.astype(F32)).astype(BF16)


def silu(x):
    return x * jax.nn.sigmoid(x)


def call(body, outs, *args, scratch=(), hbm=(), vmem=(), flops=0, name=None):
    here, far_spec = pl.BlockSpec(memory_space=pltpu.VMEM), pl.BlockSpec(memory_space=pltpu.HBM)
    size = sum(a.size * a.dtype.itemsize for a in args)
    held = {i: pltpu.HBM for i in hbm} | {i: pltpu.VMEM for i in vmem}
    args = [pltpu.with_memory_space_constraint(a, held[i]) if i in held else a for i, a in enumerate(args)]
    made = pl.pallas_call(
        body,
        out_shape=[place(o.shape, o.dtype) if place else o for o, place in outs],
        in_specs=[far_spec if i in hbm else here for i in range(len(args))],
        out_specs=[far_spec if place is pltpu.HBM else here for _, place in outs],
        scratch_shapes=list(scratch),
        compiler_params=pltpu.CompilerParams(vmem_limit_bytes=VMEM_CAP),
        cost_estimate=pl.CostEstimate(flops=flops, bytes_accessed=size, transcendentals=0),
        name=name,
    )(*args)
    return made[0] if len(outs) == 1 else made


def near(shape, dtype):
    return jax.ShapeDtypeStruct(shape, dtype), pltpu.VMEM


def far(shape, dtype):
    return jax.ShapeDtypeStruct(shape, dtype), pltpu.HBM


def free(shape, dtype):
    return jax.ShapeDtypeStruct(shape, dtype), None


def iota(shape, dim):
    return lax.broadcasted_iota(jnp.int32, shape, dim)


def dot3(a, b, ca=1, cb=0):
    ah, al = split(a)
    bh, bl = split(b)
    return dotb(jnp.concatenate([ah, al, ah], axis=ca), jnp.concatenate([bh, bh, bl], axis=cb), ca, cb)


def rim_kernel(qk_hbm, v_hbm, rim_ref, qk_ref, v_ref, sem):
    tail = pl.ds(L - 8, 8)
    copies = [
        pltpu.make_async_copy(qk_hbm.at[tail], qk_ref, sem.at[0]),
        pltpu.make_async_copy(v_hbm.at[tail], v_ref, sem.at[1]),
    ]
    for copy in copies:
        copy.start()
    for copy in copies:
        copy.wait()
    kw = qk_ref.shape[2]
    for z in range(2):
        rim_ref[:, z * kw : (z + 1) * kw] = qk_ref[:, z, :]
    rim_ref[:, 2 * kw :] = v_ref[...]


def prep_kernel(qk_hbm, v_hbm, cqk_hbm, cv_hbm, decay_hbm, beta_hbm, doc_hbm, conv_ref, edge_ref, within_ref, sys_ref, cols_ref, qk_ref, v_ref, cqk_ref, cv_ref, db_ref, doc_ref, sem):
    kw = qk_hbm.shape[2]
    vw = v_hbm.shape[1]
    pairs = (
        (doc_hbm, doc_ref),
        (decay_hbm, db_ref.at[0]),
        (beta_hbm, db_ref.at[1]),
        (cqk_hbm, cqk_ref),
        (cv_hbm, cv_ref),
        (qk_hbm, qk_ref),
        (v_hbm, v_ref),
    )
    copies = [pltpu.make_async_copy(src, dst, sem.at[i]) for i, (src, dst) in enumerate(pairs)]
    for copy in copies:
        copy.start()
    for copy in copies[:3]:
        copy.wait()
    me = lax.axis_index("seq")
    cur = doc_ref[pl.ds(me, 1), :]
    prev = doc_ref[pl.ds(jnp.maximum(me - 1, 0), 1), :]
    prev = jnp.where(me == 0, -1, prev)
    cur8 = jnp.broadcast_to(cur, (8, L)).astype(F32)
    prev8 = jnp.broadcast_to(prev, (8, L)).astype(F32)
    lane8 = iota((8, L), 1)
    row8 = iota((8, L), 0)
    cum = db_ref[0]
    for step in (1, 2, 4, 8, 16, 32, 64):
        cum = cum + jnp.where(lane8 >= step, pltpu.roll(cum, step, 1), 0.0)
    flags = (cur8 == prev8[:, L - 1 :]).astype(F32)
    for s in (1, 2, 3):
        shifted = jnp.where(lane8 < s, pltpu.roll(prev8, s, 1), pltpu.roll(cur8, s, 1))
        flags = jnp.where(row8 == s, (shifted == cur8).astype(F32), flags)
    flags = jnp.where(row8 == 4, cur8, flags)
    last = L - 1
    doc_row = cur8[:1]
    end_same = cur8 == cur8[:, last:]
    carried = jnp.exp(cum) * (cur8 == prev8[:, last:]).astype(F32)
    ends = jnp.where(end_same, jnp.exp(jnp.where(end_same, cum[:, last:] - cum, 0.0)), 0.0)
    rows = jnp.concatenate([cum, db_ref[1], flags, carried, ends, jnp.zeros((L - 40, L), F32)], axis=0)
    cols = rows.T
    cols_ref[...] = cols
    doc_col = cols[:, 20:21]
    ri, ci = iota((L, L), 0), iota((L, L), 1)
    keep = (doc_col == doc_row) & (ri >= ci)
    strict = ri > ci
    for h in range(HEADS):
        spread = cols[:, h : h + 1] - cum[h : h + 1]
        within = jnp.where(keep, jnp.exp(jnp.where(keep, spread, 0.0)), 0.0)
        within_ref[h] = within
        sys_ref[h] = jnp.where(strict, cols[:, 8 + h : 9 + h] * within, 0.0)
    for copy in copies[3:]:
        copy.wait()

    def taps(i, at, half):
        if half is None:
            return cv_ref[i : i + 1, at]
        return cqk_ref[i, half : half + 1, at]

    step = 256
    for start in range(0, 2 * kw + vw, step):
        if start < 2 * kw:
            half, off = start // kw, start % kw
        else:
            half, off = None, start - 2 * kw
        at, here = slice(off, off + step), slice(start, start + step)
        x = (v_ref[:, at] if half is None else qk_ref[:, half, at]).astype(F32)
        row = iota((8, step), 0)
        total = taps(3, at, half) * x
        for s in (1, 2, 3):
            moved = pltpu.roll(x, s, 0)
            moved = jnp.concatenate([jnp.where(row < s, 0.0, moved[:8]), moved[8:]], axis=0)
            total = total + taps(3 - s, at, half) * (moved * cols[:, 16 + s : 17 + s])
            edge_ref[8 + s : 9 + s, here] = taps(3 - s, at, half)
        edge_ref[:8, here] = total[:8]
        conv_ref[:, here] = silu(total)


def maps_kernel(conv_ref, edge_ref, halo_ref, within_ref, sys_ref, cols_ref, maps_ref, sc_ref, uw_ref, cq_ref):
    cols = cols_ref[...]
    halo = halo_ref[...].astype(F32)
    row8 = iota(halo.shape, 0)
    first = edge_ref[:8]
    for s in (1, 2, 3):
        moved = jnp.where(row8 < s, pltpu.roll(halo, s, 0), 0.0)
        first = first + edge_ref[8 + s : 9 + s] * (moved * cols[:8, 16 + s : 17 + s])
    first = silu(first)

    def feature(j):
        at = slice(j * HD, (j + 1) * HD)
        return jnp.concatenate([first[:, at], conv_ref[8:, at]], axis=0)

    ri, ci = iota((L, L), 0), iota((L, L), 1)
    eye = (ri == ci).astype(F32)
    pairs = HEADS // 2
    q_heads, k_heads, kk, qk = [], [], [], []
    for j in range(pairs):
        qj, kj = feature(j), feature(pairs + j)
        qj = qj * lax.rsqrt(jnp.sum(qj * qj, axis=1, keepdims=True) + 1e-06) * (HD ** -0.5)
        kj = kj * lax.rsqrt(jnp.sum(kj * kj, axis=1, keepdims=True) + 1e-06)
        q_heads.append(qj)
        k_heads.append(kj)
        dots = dot3(jnp.concatenate([qj, kj], axis=0), kj, 1, 1)
        qk.append(dots[:L])
        kk.append(dots[L:])
    systems = [sys_ref[h] * kk[h // 2] for h in range(HEADS)]
    narrow = [a.astype(BF16) for a in systems]
    zero = jnp.zeros((L, L), BF16)
    one = ri // 2 == ci // 2
    inverses = [eye - jnp.where(one, a, 0.0) for a in systems]
    size = 2
    while size < L:
        pick = (ri // (2 * size) == ci // (2 * size)) & (ri // size != ci // size)
        low = [x.astype(BF16) for x in inverses]
        inner = [dotb(jnp.where(pick, a, zero), x) for a, x in zip(narrow, low)]
        inverses = [x - dotb(b, y.astype(BF16)) for x, b, y in zip(inverses, low, inner)]
        size *= 2
    rests = [eye - x - dot3(a, x) for a, x in zip(systems, inverses)]
    inverses = [x + dotb(x.astype(BF16), r.astype(BF16)) for x, r in zip(inverses, rests)]
    for h in range(HEADS):
        kj = k_heads[h // 2]
        b_col = cols[:, 8 + h : 9 + h]
        carried = cols[:, 24 + h : 25 + h]
        right = jnp.concatenate([b_col * feature(2 * pairs + h), (b_col * carried) * kj], axis=1)
        uw = dot3(inverses[h], right)
        uw_ref[h] = uw
        sc_ref[h] = qk[h // 2] * within_ref[h]
        cq_ref[h] = carried * q_heads[h // 2]
        ends = dot3(cols[:, 32 + h : 33 + h] * kj, uw, 0, 0)
        maps_ref[h, :L] = (carried[L - 1 :] * eye - ends[:, HD:]).astype(BF16)
        maps_ref[h, L:] = ends[:, :HD].astype(BF16)


def local_kernel(sc_ref, uw_ref, cq_ref, out_ref, qe_ref):
    for h in range(HEADS):
        both = dot3(sc_ref[h], uw_ref[h])
        out_ref[h] = both[:, :HD]
        hi, lo = split(cq_ref[h] - both[:, HD:])
        qe_ref[h, :, :HD] = hi
        qe_ref[h, :, HD:] = lo


def chain_kernel(maps_ref, pq_ref, end_ref):
    ri, ci = iota((HD, HD), 0), iota((HD, HD), 1)
    state = jnp.concatenate([jnp.zeros((HD, HD), F32), (ri == ci).astype(F32)], axis=1)
    for i in range(RUN):
        pq_ref[i] = state
        at = RUN_ORDER.index(i)
        trans = maps_ref[at, :HD]
        offset = maps_ref[at, HD:].astype(F32)
        if i == 0:
            state = jnp.concatenate([offset, trans.astype(F32)], axis=1)
            continue
        hi, lo = split(state)
        moved = dotb(jnp.concatenate([trans, trans], axis=1), jnp.concatenate([hi, lo], axis=0))
        state = jnp.concatenate([moved[:, :HD] + offset, moved[:, HD:]], axis=1)
    end_ref[...] = state[:, :HD].astype(BF16)


def starts_kernel(pq_ref, end_ref, start_ref):
    end = end_ref[...]
    ends = jnp.concatenate([end, end], axis=0)
    for i in range(RUN):
        hi, lo = split(pq_ref[i, :, HD:])
        moved = dotb(jnp.concatenate([hi, lo], axis=1), ends)
        start_ref[RUN_ORDER.index(i)] = (pq_ref[i, :, :HD] + moved).astype(BF16)


def project_kernel(out_ref, qe_ref, start_ref, z_ref, gain_ref, w_ref, own_ref, s1_ref, s2_ref, s3_ref, part_ref):
    gain = gain_ref[...]
    gated = []
    for h in range(HEADS):
        start = start_ref[h]
        attn = out_ref[h] + dotb(qe_ref[h], jnp.concatenate([start, start], axis=0))
        z = z_ref[:, h * HD : (h + 1) * HD].astype(F32)
        scale = lax.rsqrt(jnp.mean(attn * attn, axis=1, keepdims=True) + 1e-06)
        gated.append((attn * scale * gain * silu(z)).astype(BF16))
    part_ref[...] = dotb(jnp.concatenate(gated, axis=1), w_ref[...])
    me = lax.axis_index("exp")
    n = own_ref.shape[0]
    own_ref[...] = part_ref[pl.ds(pl.multiple_of(me * n, n), n)]
    for s, ref in ((1, s1_ref), (2, s2_ref), (3, s3_ref)):
        to = lax.rem(me + s, 4)
        ref[...] = part_ref[pl.ds(pl.multiple_of(to * n, n), n)].astype(BF16)


def route_kernel(own_ref, r1_ref, r2_ref, r3_ref, res_ref, gain_ref, ids_ref, wt_ref, to_ref, mid_ref, norm_ref, send_ref, pick_ref):
    hidden = own_ref[...] + r1_ref[...].astype(F32) + r2_ref[...].astype(F32) + r3_ref[...].astype(F32)
    hidden = res_ref[...].astype(F32) + hidden
    mid_ref[...] = hidden.astype(BF16)
    normed = hidden * lax.rsqrt(jnp.mean(hidden * hidden, axis=1, keepdims=True) + 1e-06) * gain_ref[...]
    normed = normed.astype(BF16)
    norm_ref[...] = normed
    tokens, width = normed.shape
    half = width // 2
    slots = send_ref.shape[0]
    col = iota((tokens, slots), 1)
    rank = (col // 2) % 2
    named = jnp.zeros((tokens, slots), F32)
    weight = jnp.zeros((tokens, slots), F32)
    ti, tj = iota((tokens, tokens), 0), iota((tokens, tokens), 1)
    same = (ti == tj).astype(F32)
    ids = dotf(same, ids_ref[...].astype(F32), 1, 1)
    weights = dotf(same, wt_ref[...], 1, 1)
    expert = to_ref[...].astype(F32)
    for k in range(ids_ref.shape[0]):
        hit = expert == ids[:, k : k + 1]
        named = jnp.where(hit, 1.0, named)
        weight = jnp.where(hit, weights[:, k : k + 1], weight)
    before = (ti > tj).astype(BF16)
    earlier = dotb(before, named.astype(BF16))
    chosen = jnp.where(earlier == rank.astype(F32), named, 0.0)
    weight = chosen * weight
    low = col % 2 == 0
    pick = jnp.concatenate([jnp.where(low, chosen, 0.0), jnp.where(low, 0.0, chosen)], axis=0).astype(BF16)
    send_ref[...] = dotb(pick, jnp.concatenate([normed[:, :half], normed[:, half:]], axis=0), 0, 0).astype(BF16)
    both = jnp.concatenate([jnp.where(low, weight, 0.0), jnp.where(low, 0.0, weight)], axis=0)
    hi, lo = split(both)
    pick_ref[: 2 * tokens] = hi
    pick_ref[2 * tokens :] = lo


def shared_kernel(norm_ref, gate_ref, sgu_hbm, sdown_hbm, out_ref, sgu_ref, sdown_ref, sem):
    pairs = ((sgu_hbm, sgu_ref), (sdown_hbm, sdown_ref))
    copies = [pltpu.make_async_copy(src, dst, sem.at[i]) for i, (src, dst) in enumerate(pairs)]
    for copy in copies:
        copy.start()
    normed = norm_ref[...]
    score = jnp.sum(normed.astype(F32) * gate_ref[...], axis=1, keepdims=True)
    copies[0].wait()
    act = (silu(dotb(normed, sgu_ref[0])) * dotb(normed, sgu_ref[1])).astype(BF16)
    copies[1].wait()
    out_ref[...] = jax.nn.sigmoid(score) * dotb(act, sdown_ref[...])


def fetch_kernel(gu_hbm, down_hbm, gu_ref, down_ref, sem):
    copies = [
        pltpu.make_async_copy(src.at[e], dst.at[e], sem.at[2 * i + e])
        for i, (src, dst) in enumerate(((gu_hbm, gu_ref), (down_hbm, down_ref)))
        for e in range(2)
    ]
    for copy in copies:
        copy.start()
    for copy in copies:
        copy.wait()


def expert_kernel(recv_ref, gu_ref, down_ref, out_hbm, flat_ref, made_ref, x0_ref, x1_ref, out_ref, sem):
    rows, half = recv_ref.shape
    srcs = rows // 8
    flat = functools.partial(pl.ds, size=srcs, stride=8)
    lanes, wide = 128, 256
    x_refs = (x0_ref, x1_ref)

    def gather(e, c):
        for r in range(2):
            for b in range(2):
                to = slice(b * half + c * lanes, b * half + (c + 1) * lanes)
                x_refs[e][r * srcs : (r + 1) * srcs, to] = flat_ref[c, flat(4 * e + 2 * r + b), :].astype(BF16)

    def down(e, act, p):
        for b in range(2):
            y = dotb(act, down_ref[e, :, b * half + p * wide : b * half + (p + 1) * wide])
            for r in range(2):
                for c in range(2):
                    made_ref[2 * p + c, flat(4 * e + 2 * r + b), :] = y[r * srcs : (r + 1) * srcs, c * lanes : (c + 1) * lanes]

    def hidden(e, n):
        at = slice(n * wide, (n + 1) * wide)
        x = x_refs[e][...]
        return (silu(dotb(x, gu_ref[e, 0, :, at])) * dotb(x, gu_ref[e, 1, :, at])).astype(BF16)

    for c in range(half // lanes):
        flat_ref[c] = recv_ref[:, c * lanes : (c + 1) * lanes].astype(F32)
        gather(0, c)
    parts = gu_ref.shape[3] // wide
    per = half // lanes // parts
    acts = []
    for n in range(parts):
        acts.append(hidden(0, n))
        for c in range(n * per, (n + 1) * per):
            gather(1, c)
    first = jnp.concatenate(acts, axis=1)
    acts = []
    share = half // wide // parts
    for n in range(parts):
        acts.append(hidden(1, n))
        for p in range(n * share, (n + 1) * share):
            down(0, first, p)
    second = jnp.concatenate(acts, axis=1)
    copies = []
    for p in range(half // wide):
        down(1, second, p)
        for c in (2 * p, 2 * p + 1):
            out_ref[:, c * lanes : (c + 1) * lanes] = made_ref[c].astype(BF16)
        at = slice(p * wide, (p + 1) * wide)
        copies.append(pltpu.make_async_copy(out_ref.at[:, at], out_hbm.at[:, at], sem.at[p]))
        copies[-1].start()
    for copy in copies:
        copy.wait()


def combine_kernel(back_ref, pick_ref, shared_ref, out_ref):
    got = dotb(pick_ref[...], back_ref[...])
    n = got.shape[0] // 4
    half = got.shape[1]
    got = got[: 2 * n] + got[2 * n :]
    out_ref[:, :half] = (got[:n] + shared_ref[:, :half]).astype(BF16)
    out_ref[:, half:] = (got[n:] + shared_ref[:, half:]).astype(BF16)


def exchange_order(seq_n, exp_n):
    return [s * exp_n + e for c in range(2) for s in range(c, seq_n, 2) for e in range(exp_n)]


def shards(
    qk_proj,
    v_proj,
    z_proj,
    conv_qk,
    conv_v,
    decay_log,
    beta_gate,
    doc_ids,
    head_gain,
    out_weight,
    residual,
    post_gain,
    route_ids,
    route_weight,
    expert_gate_up,
    expert_down,
    shared_gate_up,
    shared_down,
    shared_gate,
):
    seq_n, exp_n = lax.axis_size("seq"), lax.axis_size("exp")
    runs = [[g * RUN + i for i in RUN_ORDER] for g in range(seq_n // RUN)]
    kw, vw = qk_proj.shape[2], v_proj.shape[1]
    wide = 2 * kw + vw
    rim = call(
        rim_kernel,
        (near((8, wide), BF16),),
        qk_proj, v_proj,
        hbm=(0, 1),
        scratch=[pltpu.VMEM((8, 2, kw), BF16), pltpu.VMEM((8, vw), BF16), pltpu.SemaphoreType.DMA((2,))],
        name="rim",
    )
    halo = lax.ppermute(rim, "seq", [(i, i + 1) for i in range(seq_n - 1)])

    conv, edge, within, system, cols = call(
        prep_kernel,
        (
            near((L, wide), F32),
            near((16, wide), F32),
            near((HEADS, L, L), F32),
            near((HEADS, L, L), F32),
            near((L, L), F32),
        ),
        qk_proj, v_proj, conv_qk, conv_v, decay_log, beta_gate, doc_ids.reshape(seq_n, L),
        hbm=range(7),
        scratch=[
            pltpu.VMEM((L, 2, kw), BF16),
            pltpu.VMEM((L, vw), BF16),
            pltpu.VMEM(conv_qk.shape, F32),
            pltpu.VMEM(conv_v.shape, F32),
            pltpu.VMEM((2, HEADS, L), F32),
            pltpu.VMEM((seq_n, L), jnp.int32),
            pltpu.SemaphoreType.DMA((7,)),
        ],
        flops=10**8,
        name="prep",
    )
    maps, scores, uw, cq = call(
        maps_kernel,
        (
            near((HEADS, 2 * HD, HD), BF16),
            near((HEADS, L, L), F32),
            near((HEADS, L, 2 * HD), F32),
            near((HEADS, L, HD), F32),
        ),
        conv, edge, halo, within, system, cols,
        flops=2 * 10**9,
        name="maps",
    )
    maps = lax.all_to_all(maps, "seq", split_axis=0, concat_axis=0, tiled=True, axis_index_groups=runs)
    local_out, query_eff = call(
        local_kernel,
        (near((HEADS, L, HD), F32), near((HEADS, L, 2 * HD), BF16)),
        scores, uw, cq,
        flops=10**8,
        name="local_out",
    )
    pq, end = call(
        chain_kernel,
        (near((RUN, HD, 2 * HD), F32), near((HD, HD), BF16)),
        maps,
        flops=10**8,
        name="chain",
    )
    end = lax.ppermute(end, "seq", [(i, i + RUN) for i in range(seq_n - RUN)])
    end, local_out, query_eff = lax.optimization_barrier((end, local_out, query_eff))
    starts = call(starts_kernel, (near((RUN, HD, HD), BF16),), pq, end, flops=10**8, name="starts")
    starts = lax.all_to_all(starts, "seq", split_axis=0, concat_axis=0, tiled=True, axis_index_groups=runs)

    model = out_weight.shape[1]
    rows = residual.shape[0]
    piece = near((rows, model), BF16)
    own, *sends = call(
        project_kernel,
        (near((rows, model), F32), piece, piece, piece),
        local_out, query_eff, starts, z_proj, head_gain.reshape(1, HD), out_weight,
        vmem=(3, 5),
        scratch=[pltpu.VMEM((L, model), F32)],
        flops=6 * 10**8,
        name="project",
    )
    got = {}
    for s in (2, 1, 3):
        got[s] = lax.ppermute(sends[s - 1], "exp", [(i, (i + s) % exp_n) for i in range(exp_n)])
    gu_near, down_near = call(
        fetch_kernel,
        (near(expert_gate_up.shape, BF16), near(expert_down.shape, BF16)),
        expert_gate_up, expert_down,
        hbm=(0, 1),
        scratch=[pltpu.SemaphoreType.DMA((4,))],
        name="fetch",
    )
    own, gu_near, down_near = lax.optimization_barrier((own, gu_near, down_near))
    devices = seq_n * exp_n
    slots = devices * 8
    half = model // 2
    order = exchange_order(seq_n, exp_n)
    experts_at = np.repeat(2 * np.asarray(order, np.int32), 8).reshape(1, slots)
    experts_at = experts_at + (np.arange(slots, dtype=np.int32) // 4 % 2)
    hidden_mid, normed, send, pick = call(
        route_kernel,
        (free((rows, model), BF16), piece, near((slots, half), BF16), near((4 * rows, slots), BF16)),
        own, got[1], got[2], got[3], residual, post_gain.reshape(1, model), route_ids.T, route_weight.T, jnp.asarray(experts_at),
        flops=2 * 10**8,
        name="route",
    )
    axes = ("seq", "exp")
    recv = lax.all_to_all(send.reshape(devices, 8, half), axes, split_axis=0, concat_axis=0, tiled=True, axis_index_groups=[order])
    made = call(
        expert_kernel,
        (far((slots, half), BF16),),
        recv.reshape(slots, half), gu_near, down_near,
        scratch=[
            pltpu.VMEM((half // 128, slots, 128), F32),
            pltpu.VMEM((half // 128, slots, 128), F32),
            pltpu.VMEM((2 * devices, model), BF16),
            pltpu.VMEM((2 * devices, model), BF16),
            pltpu.VMEM((slots, half), BF16),
            pltpu.SemaphoreType.DMA((half // 256,)),
        ],
        flops=4 * 10**9,
        name="experts",
    )
    made, normed = lax.optimization_barrier((made, normed))
    shared = call(
        shared_kernel,
        (near((rows, model), F32),),
        normed, shared_gate.reshape(1, model), shared_gate_up, shared_down,
        hbm=(2, 3),
        scratch=[
            pltpu.VMEM(shared_gate_up.shape, BF16),
            pltpu.VMEM(shared_down.shape, BF16),
            pltpu.SemaphoreType.DMA((2,)),
        ],
        flops=2 * 10**8,
        name="shared",
    )
    back = lax.all_to_all(made.reshape(devices, 8, half), axes, split_axis=0, concat_axis=0, tiled=True, axis_index_groups=[order])
    moe_out = call(
        combine_kernel,
        (free((rows, model), BF16),),
        back.reshape(slots, half), pick, shared,
        flops=3 * 10**8,
        name="combine",
    )
    return hidden_mid, moe_out


def solution(mesh):
    placed = (
        P("seq", None, "exp"),
        P("seq", "exp"),
        P("seq", "exp"),
        P(None, None, "exp"),
        P(None, "exp"),
        P("exp", "seq"),
        P("exp", "seq"),
        P(),
        P(),
        P("exp", None),
        P(("seq", "exp"), None),
        P(),
        P(("seq", "exp"), None),
        P(("seq", "exp"), None),
        P(("seq", "exp"), None, None, None),
        P(("seq", "exp"), None, None),
        P(),
        P(),
        P(),
    )
    return jax.shard_map(
        shards,
        mesh=mesh,
        in_specs=placed,
        out_specs=(P(("seq", "exp"), None), P(("seq", "exp"), None)),
        check_vma=False,
    )
```

```python
import functools

import jax
import jax.numpy as jnp
import numpy as np
from jax import lax
from jax.experimental import pallas as pl
from jax.experimental.pallas import tpu as pltpu
from jax.sharding import PartitionSpec as P

F32 = jnp.float32
BF16 = jnp.bfloat16
HIGH = lax.Precision.HIGHEST
L = 128
HD = 128
HEADS = 8
RUN = 8
RUN_ORDER = (0, 2, 4, 6, 1, 3, 5, 7)
VMEM_CAP = 28 * 1024 * 1024


def dotf(a, b, ca=1, cb=0):
    return lax.dot_general(a, b, (((ca,), (cb,)), ((), ())), precision=HIGH, preferred_element_type=F32)


def dotb(a, b, ca=1, cb=0):
    return lax.dot_general(a, b, (((ca,), (cb,)), ((), ())), preferred_element_type=F32)


def split(x):
    hi = x.astype(BF16)
    return hi, (x - hi.astype(F32)).astype(BF16)


def silu(x):
    return x * jax.nn.sigmoid(x)


def call(body, outs, *args, scratch=(), hbm=(), vmem=(), flops=0, name=None):
    here, far_spec = pl.BlockSpec(memory_space=pltpu.VMEM), pl.BlockSpec(memory_space=pltpu.HBM)
    size = sum(a.size * a.dtype.itemsize for a in args)
    held = {i: pltpu.HBM for i in hbm} | {i: pltpu.VMEM for i in vmem}
    args = [pltpu.with_memory_space_constraint(a, held[i]) if i in held else a for i, a in enumerate(args)]
    made = pl.pallas_call(
        body,
        out_shape=[place(o.shape, o.dtype) if place else o for o, place in outs],
        in_specs=[far_spec if i in hbm else here for i in range(len(args))],
        out_specs=[far_spec if place is pltpu.HBM else here for _, place in outs],
        scratch_shapes=list(scratch),
        compiler_params=pltpu.CompilerParams(vmem_limit_bytes=VMEM_CAP),
        cost_estimate=pl.CostEstimate(flops=flops, bytes_accessed=size, transcendentals=0),
        name=name,
    )(*args)
    return made[0] if len(outs) == 1 else made


def near(shape, dtype):
    return jax.ShapeDtypeStruct(shape, dtype), pltpu.VMEM


def far(shape, dtype):
    return jax.ShapeDtypeStruct(shape, dtype), pltpu.HBM


def free(shape, dtype):
    return jax.ShapeDtypeStruct(shape, dtype), None


def iota(shape, dim):
    return lax.broadcasted_iota(jnp.int32, shape, dim)


def dot3(a, b, ca=1, cb=0):
    ah, al = split(a)
    bh, bl = split(b)
    return dotb(jnp.concatenate([ah, al, ah], axis=ca), jnp.concatenate([bh, bh, bl], axis=cb), ca, cb)


def rim_kernel(qk_hbm, v_hbm, rim_ref, qk_ref, v_ref, sem):
    tail = pl.ds(L - 8, 8)
    copies = [
        pltpu.make_async_copy(qk_hbm.at[tail], qk_ref, sem.at[0]),
        pltpu.make_async_copy(v_hbm.at[tail], v_ref, sem.at[1]),
    ]
    for copy in copies:
        copy.start()
    for copy in copies:
        copy.wait()
    kw = qk_ref.shape[2]
    for z in range(2):
        rim_ref[:, z * kw : (z + 1) * kw] = qk_ref[:, z, :]
    rim_ref[:, 2 * kw :] = v_ref[...]


def prep_kernel(qk_hbm, v_hbm, cqk_hbm, cv_hbm, decay_hbm, beta_hbm, doc_hbm, conv_ref, edge_ref, within_ref, sys_ref, cols_ref, qk_ref, v_ref, cqk_ref, cv_ref, db_ref, doc_ref, sem):
    kw = qk_hbm.shape[2]
    vw = v_hbm.shape[1]
    pairs = (
        (doc_hbm, doc_ref),
        (decay_hbm, db_ref.at[0]),
        (beta_hbm, db_ref.at[1]),
        (cqk_hbm, cqk_ref),
        (cv_hbm, cv_ref),
        (qk_hbm, qk_ref),
        (v_hbm, v_ref),
    )
    copies = [pltpu.make_async_copy(src, dst, sem.at[i]) for i, (src, dst) in enumerate(pairs)]
    for copy in copies:
        copy.start()
    for copy in copies[:3]:
        copy.wait()
    me = lax.axis_index("seq")
    cur = doc_ref[pl.ds(me, 1), :]
    prev = doc_ref[pl.ds(jnp.maximum(me - 1, 0), 1), :]
    prev = jnp.where(me == 0, -1, prev)
    cur8 = jnp.broadcast_to(cur, (8, L)).astype(F32)
    prev8 = jnp.broadcast_to(prev, (8, L)).astype(F32)
    lane8 = iota((8, L), 1)
    row8 = iota((8, L), 0)
    cum = db_ref[0]
    for step in (1, 2, 4, 8, 16, 32, 64):
        cum = cum + jnp.where(lane8 >= step, pltpu.roll(cum, step, 1), 0.0)
    flags = (cur8 == prev8[:, L - 1 :]).astype(F32)
    for s in (1, 2, 3):
        shifted = jnp.where(lane8 < s, pltpu.roll(prev8, s, 1), pltpu.roll(cur8, s, 1))
        flags = jnp.where(row8 == s, (shifted == cur8).astype(F32), flags)
    flags = jnp.where(row8 == 4, cur8, flags)
    last = L - 1
    doc_row = cur8[:1]
    end_same = cur8 == cur8[:, last:]
    carried = jnp.exp(cum) * (cur8 == prev8[:, last:]).astype(F32)
    ends = jnp.where(end_same, jnp.exp(jnp.where(end_same, cum[:, last:] - cum, 0.0)), 0.0)
    rows = jnp.concatenate([cum, db_ref[1], flags, carried, ends, jnp.zeros((L - 40, L), F32)], axis=0)
    cols = rows.T
    cols_ref[...] = cols
    doc_col = cols[:, 20:21]
    ri, ci = iota((L, L), 0), iota((L, L), 1)
    keep = (doc_col == doc_row) & (ri >= ci)
    strict = ri > ci
    for h in range(HEADS):
        spread = cols[:, h : h + 1] - cum[h : h + 1]
        within = jnp.where(keep, jnp.exp(jnp.where(keep, spread, 0.0)), 0.0)
        within_ref[h] = within
        sys_ref[h] = jnp.where(strict, cols[:, 8 + h : 9 + h] * within, 0.0)
    for copy in copies[3:]:
        copy.wait()

    def taps(i, at, half):
        if half is None:
            return cv_ref[i : i + 1, at]
        return cqk_ref[i, half : half + 1, at]

    step = 256
    for start in range(0, 2 * kw + vw, step):
        if start < 2 * kw:
            half, off = start // kw, start % kw
        else:
            half, off = None, start - 2 * kw
        at, here = slice(off, off + step), slice(start, start + step)
        x = (v_ref[:, at] if half is None else qk_ref[:, half, at]).astype(F32)
        row = iota((8, step), 0)
        total = taps(3, at, half) * x
        for s in (1, 2, 3):
            moved = pltpu.roll(x, s, 0)
            moved = jnp.concatenate([jnp.where(row < s, 0.0, moved[:8]), moved[8:]], axis=0)
            total = total + taps(3 - s, at, half) * (moved * cols[:, 16 + s : 17 + s])
            edge_ref[8 + s : 9 + s, here] = taps(3 - s, at, half)
        edge_ref[:8, here] = total[:8]
        conv_ref[:, here] = silu(total)


def maps_kernel(conv_ref, edge_ref, halo_ref, within_ref, sys_ref, cols_ref, maps_ref, sc_ref, uw_ref, cq_ref):
    cols = cols_ref[...]
    halo = halo_ref[...].astype(F32)
    row8 = iota(halo.shape, 0)
    first = edge_ref[:8]
    for s in (1, 2, 3):
        moved = jnp.where(row8 < s, pltpu.roll(halo, s, 0), 0.0)
        first = first + edge_ref[8 + s : 9 + s] * (moved * cols[:8, 16 + s : 17 + s])
    first = silu(first)

    def feature(j):
        at = slice(j * HD, (j + 1) * HD)
        return jnp.concatenate([first[:, at], conv_ref[8:, at]], axis=0)

    ri, ci = iota((L, L), 0), iota((L, L), 1)
    eye = (ri == ci).astype(F32)
    pairs = HEADS // 2
    q_heads, k_heads, kk, qk = [], [], [], []
    for j in range(pairs):
        qj, kj = feature(j), feature(pairs + j)
        qj = qj * lax.rsqrt(jnp.sum(qj * qj, axis=1, keepdims=True) + 1e-06) * (HD ** -0.5)
        kj = kj * lax.rsqrt(jnp.sum(kj * kj, axis=1, keepdims=True) + 1e-06)
        q_heads.append(qj)
        k_heads.append(kj)
        dots = dot3(jnp.concatenate([qj, kj], axis=0), kj, 1, 1)
        qk.append(dots[:L])
        kk.append(dots[L:])
    systems = [sys_ref[h] * kk[h // 2] for h in range(HEADS)]
    narrow = [a.astype(BF16) for a in systems]
    zero = jnp.zeros((L, L), BF16)
    one = ri // 2 == ci // 2
    inverses = [eye - jnp.where(one, a, 0.0) for a in systems]
    size = 2
    while size < L:
        pick = (ri // (2 * size) == ci // (2 * size)) & (ri // size != ci // size)
        low = [x.astype(BF16) for x in inverses]
        inner = [dotb(jnp.where(pick, a, zero), x) for a, x in zip(narrow, low)]
        inverses = [x - dotb(b, y.astype(BF16)) for x, b, y in zip(inverses, low, inner)]
        size *= 2
    rests = [eye - x - dot3(a, x) for a, x in zip(systems, inverses)]
    inverses = [x + dotb(x.astype(BF16), r.astype(BF16)) for x, r in zip(inverses, rests)]
    for h in range(HEADS):
        kj = k_heads[h // 2]
        b_col = cols[:, 8 + h : 9 + h]
        carried = cols[:, 24 + h : 25 + h]
        right = jnp.concatenate([b_col * feature(2 * pairs + h), (b_col * carried) * kj], axis=1)
        uw = dot3(inverses[h], right)
        uw_ref[h] = uw
        sc_ref[h] = qk[h // 2] * within_ref[h]
        cq_ref[h] = carried * q_heads[h // 2]
        ends = dotb((cols[:, 32 + h : 33 + h] * kj).astype(BF16), uw.astype(BF16), 0, 0)
        maps_ref[h, :L] = (carried[L - 1 :] * eye - ends[:, HD:]).astype(BF16)
        maps_ref[h, L:] = ends[:, :HD].astype(BF16)


def local_kernel(sc_ref, uw_ref, cq_ref, out_ref, qe_ref):
    for h in range(HEADS):
        both = dot3(sc_ref[h], uw_ref[h])
        out_ref[h] = both[:, :HD]
        hi, lo = split(cq_ref[h] - both[:, HD:])
        qe_ref[h, :, :HD] = hi
        qe_ref[h, :, HD:] = lo


def chain_kernel(maps_ref, pq_ref, end_ref):
    ri, ci = iota((HD, HD), 0), iota((HD, HD), 1)
    state = jnp.concatenate([jnp.zeros((HD, HD), F32), (ri == ci).astype(F32)], axis=1)
    for i in range(RUN):
        pq_ref[i] = state
        at = RUN_ORDER.index(i)
        trans = maps_ref[at, :HD]
        offset = maps_ref[at, HD:].astype(F32)
        if i == 0:
            state = jnp.concatenate([offset, trans.astype(F32)], axis=1)
            continue
        hi, lo = split(state)
        moved = dotb(jnp.concatenate([trans, trans], axis=1), jnp.concatenate([hi, lo], axis=0))
        state = jnp.concatenate([moved[:, :HD] + offset, moved[:, HD:]], axis=1)
    end_ref[...] = state[:, :HD].astype(BF16)


def starts_kernel(pq_ref, end_ref, start_ref):
    end = end_ref[...]
    ends = jnp.concatenate([end, end], axis=0)
    for i in range(RUN):
        hi, lo = split(pq_ref[i, :, HD:])
        moved = dotb(jnp.concatenate([hi, lo], axis=1), ends)
        start_ref[RUN_ORDER.index(i)] = (pq_ref[i, :, :HD] + moved).astype(BF16)


def project_kernel(out_ref, qe_ref, start_ref, z_ref, gain_ref, w_ref, own_ref, s1_ref, s2_ref, s3_ref, part_ref):
    gain = gain_ref[...]
    gated = []
    for h in range(HEADS):
        start = start_ref[h]
        attn = out_ref[h] + dotb(qe_ref[h], jnp.concatenate([start, start], axis=0))
        z = z_ref[:, h * HD : (h + 1) * HD].astype(F32)
        scale = lax.rsqrt(jnp.mean(attn * attn, axis=1, keepdims=True) + 1e-06)
        gated.append((attn * scale * gain * silu(z)).astype(BF16))
    part_ref[...] = dotb(jnp.concatenate(gated, axis=1), w_ref[...])
    me = lax.axis_index("exp")
    n = own_ref.shape[0]
    own_ref[...] = part_ref[pl.ds(pl.multiple_of(me * n, n), n)]
    for s, ref in ((1, s1_ref), (2, s2_ref), (3, s3_ref)):
        to = lax.rem(me + s, 4)
        ref[...] = part_ref[pl.ds(pl.multiple_of(to * n, n), n)].astype(BF16)


def route_kernel(own_ref, r1_ref, r2_ref, r3_ref, res_ref, gain_ref, ids_ref, wt_ref, to_ref, mid_ref, norm_ref, send_ref, pick_ref):
    hidden = own_ref[...] + r1_ref[...].astype(F32) + r2_ref[...].astype(F32) + r3_ref[...].astype(F32)
    hidden = res_ref[...].astype(F32) + hidden
    mid_ref[...] = hidden.astype(BF16)
    normed = hidden * lax.rsqrt(jnp.mean(hidden * hidden, axis=1, keepdims=True) + 1e-06) * gain_ref[...]
    normed = normed.astype(BF16)
    norm_ref[...] = normed
    tokens, width = normed.shape
    half = width // 2
    slots = send_ref.shape[0]
    col = iota((tokens, slots), 1)
    rank = (col // 2) % 2
    named = jnp.zeros((tokens, slots), F32)
    weight = jnp.zeros((tokens, slots), F32)
    ti, tj = iota((tokens, tokens), 0), iota((tokens, tokens), 1)
    same = (ti == tj).astype(F32)
    ids = dotf(same, ids_ref[...].astype(F32), 1, 1)
    weights = dotf(same, wt_ref[...], 1, 1)
    expert = to_ref[...].astype(F32)
    for k in range(ids_ref.shape[0]):
        hit = expert == ids[:, k : k + 1]
        named = jnp.where(hit, 1.0, named)
        weight = jnp.where(hit, weights[:, k : k + 1], weight)
    before = (ti > tj).astype(BF16)
    earlier = dotb(before, named.astype(BF16))
    chosen = jnp.where(earlier == rank.astype(F32), named, 0.0)
    weight = chosen * weight
    low = col % 2 == 0
    pick = jnp.concatenate([jnp.where(low, chosen, 0.0), jnp.where(low, 0.0, chosen)], axis=0).astype(BF16)
    send_ref[...] = dotb(pick, jnp.concatenate([normed[:, :half], normed[:, half:]], axis=0), 0, 0).astype(BF16)
    both = jnp.concatenate([jnp.where(low, weight, 0.0), jnp.where(low, 0.0, weight)], axis=0)
    hi, lo = split(both)
    pick_ref[: 2 * tokens] = hi
    pick_ref[2 * tokens :] = lo


def shared_kernel(norm_ref, gate_ref, sgu_hbm, sdown_hbm, out_ref, sgu_ref, sdown_ref, sem):
    pairs = ((sgu_hbm, sgu_ref), (sdown_hbm, sdown_ref))
    copies = [pltpu.make_async_copy(src, dst, sem.at[i]) for i, (src, dst) in enumerate(pairs)]
    for copy in copies:
        copy.start()
    normed = norm_ref[...]
    score = jnp.sum(normed.astype(F32) * gate_ref[...], axis=1, keepdims=True)
    copies[0].wait()
    act = (silu(dotb(normed, sgu_ref[0])) * dotb(normed, sgu_ref[1])).astype(BF16)
    copies[1].wait()
    out_ref[...] = jax.nn.sigmoid(score) * dotb(act, sdown_ref[...])


def fetch_kernel(gu_hbm, down_hbm, gu_ref, down_ref, sem):
    copies = [
        pltpu.make_async_copy(src.at[e], dst.at[e], sem.at[2 * i + e])
        for i, (src, dst) in enumerate(((gu_hbm, gu_ref), (down_hbm, down_ref)))
        for e in range(2)
    ]
    for copy in copies:
        copy.start()
    for copy in copies:
        copy.wait()


def expert_kernel(recv_ref, gu_ref, down_ref, out_hbm, flat_ref, made_ref, x0_ref, x1_ref, out_ref, sem):
    rows, half = recv_ref.shape
    srcs = rows // 8
    flat = functools.partial(pl.ds, size=srcs, stride=8)
    lanes, wide = 128, 256
    x_refs = (x0_ref, x1_ref)

    def gather(e, c):
        for r in range(2):
            for b in range(2):
                to = slice(b * half + c * lanes, b * half + (c + 1) * lanes)
                x_refs[e][r * srcs : (r + 1) * srcs, to] = flat_ref[c, flat(4 * e + 2 * r + b), :].astype(BF16)

    def down(e, act, p):
        for b in range(2):
            y = dotb(act, down_ref[e, :, b * half + p * wide : b * half + (p + 1) * wide])
            for r in range(2):
                for c in range(2):
                    made_ref[2 * p + c, flat(4 * e + 2 * r + b), :] = y[r * srcs : (r + 1) * srcs, c * lanes : (c + 1) * lanes]

    def hidden(e, n):
        at = slice(n * wide, (n + 1) * wide)
        x = x_refs[e][...]
        return (silu(dotb(x, gu_ref[e, 0, :, at])) * dotb(x, gu_ref[e, 1, :, at])).astype(BF16)

    for c in range(half // lanes):
        flat_ref[c] = recv_ref[:, c * lanes : (c + 1) * lanes].astype(F32)
        gather(0, c)
    parts = gu_ref.shape[3] // wide
    per = half // lanes // parts
    acts = []
    for n in range(parts):
        acts.append(hidden(0, n))
        for c in range(n * per, (n + 1) * per):
            gather(1, c)
    first = jnp.concatenate(acts, axis=1)
    acts = []
    share = half // wide // parts
    for n in range(parts):
        acts.append(hidden(1, n))
        for p in range(n * share, (n + 1) * share):
            down(0, first, p)
    second = jnp.concatenate(acts, axis=1)
    copies = []
    for p in range(half // wide):
        down(1, second, p)
        for c in (2 * p, 2 * p + 1):
            out_ref[:, c * lanes : (c + 1) * lanes] = made_ref[c].astype(BF16)
        at = slice(p * wide, (p + 1) * wide)
        copies.append(pltpu.make_async_copy(out_ref.at[:, at], out_hbm.at[:, at], sem.at[p]))
        copies[-1].start()
    for copy in copies:
        copy.wait()


def combine_kernel(back_ref, pick_ref, shared_ref, out_ref):
    got = dotb(pick_ref[...], back_ref[...])
    n = got.shape[0] // 4
    half = got.shape[1]
    got = got[: 2 * n] + got[2 * n :]
    out_ref[:, :half] = (got[:n] + shared_ref[:, :half]).astype(BF16)
    out_ref[:, half:] = (got[n:] + shared_ref[:, half:]).astype(BF16)


def exchange_order(seq_n, exp_n):
    return [s * exp_n + e for c in range(2) for s in range(c, seq_n, 2) for e in range(exp_n)]


def shards(
    qk_proj,
    v_proj,
    z_proj,
    conv_qk,
    conv_v,
    decay_log,
    beta_gate,
    doc_ids,
    head_gain,
    out_weight,
    residual,
    post_gain,
    route_ids,
    route_weight,
    expert_gate_up,
    expert_down,
    shared_gate_up,
    shared_down,
    shared_gate,
):
    seq_n, exp_n = lax.axis_size("seq"), lax.axis_size("exp")
    runs = [[g * RUN + i for i in RUN_ORDER] for g in range(seq_n // RUN)]
    kw, vw = qk_proj.shape[2], v_proj.shape[1]
    wide = 2 * kw + vw
    rim = call(
        rim_kernel,
        (near((8, wide), BF16),),
        qk_proj, v_proj,
        hbm=(0, 1),
        scratch=[pltpu.VMEM((8, 2, kw), BF16), pltpu.VMEM((8, vw), BF16), pltpu.SemaphoreType.DMA((2,))],
        name="rim",
    )
    halo = lax.ppermute(rim, "seq", [(i, i + 1) for i in range(seq_n - 1)])

    conv, edge, within, system, cols = call(
        prep_kernel,
        (
            near((L, wide), F32),
            near((16, wide), F32),
            near((HEADS, L, L), F32),
            near((HEADS, L, L), F32),
            near((L, L), F32),
        ),
        qk_proj, v_proj, conv_qk, conv_v, decay_log, beta_gate, doc_ids.reshape(seq_n, L),
        hbm=range(7),
        scratch=[
            pltpu.VMEM((L, 2, kw), BF16),
            pltpu.VMEM((L, vw), BF16),
            pltpu.VMEM(conv_qk.shape, F32),
            pltpu.VMEM(conv_v.shape, F32),
            pltpu.VMEM((2, HEADS, L), F32),
            pltpu.VMEM((seq_n, L), jnp.int32),
            pltpu.SemaphoreType.DMA((7,)),
        ],
        flops=10**8,
        name="prep",
    )
    maps, scores, uw, cq = call(
        maps_kernel,
        (
            near((HEADS, 2 * HD, HD), BF16),
            near((HEADS, L, L), F32),
            near((HEADS, L, 2 * HD), F32),
            near((HEADS, L, HD), F32),
        ),
        conv, edge, halo, within, system, cols,
        flops=2 * 10**9,
        name="maps",
    )
    maps = lax.all_to_all(maps, "seq", split_axis=0, concat_axis=0, tiled=True, axis_index_groups=runs)
    local_out, query_eff = call(
        local_kernel,
        (near((HEADS, L, HD), F32), near((HEADS, L, 2 * HD), BF16)),
        scores, uw, cq,
        flops=10**8,
        name="local_out",
    )
    pq, end = call(
        chain_kernel,
        (near((RUN, HD, 2 * HD), F32), near((HD, HD), BF16)),
        maps,
        flops=10**8,
        name="chain",
    )
    end = lax.ppermute(end, "seq", [(i, i + RUN) for i in range(seq_n - RUN)])
    end, local_out, query_eff = lax.optimization_barrier((end, local_out, query_eff))
    starts = call(starts_kernel, (near((RUN, HD, HD), BF16),), pq, end, flops=10**8, name="starts")
    starts = lax.all_to_all(starts, "seq", split_axis=0, concat_axis=0, tiled=True, axis_index_groups=runs)

    model = out_weight.shape[1]
    rows = residual.shape[0]
    piece = near((rows, model), BF16)
    own, *sends = call(
        project_kernel,
        (near((rows, model), F32), piece, piece, piece),
        local_out, query_eff, starts, z_proj, head_gain.reshape(1, HD), out_weight,
        vmem=(3, 5),
        scratch=[pltpu.VMEM((L, model), F32)],
        flops=6 * 10**8,
        name="project",
    )
    got = {}
    for s in (2, 1, 3):
        got[s] = lax.ppermute(sends[s - 1], "exp", [(i, (i + s) % exp_n) for i in range(exp_n)])
    gu_near, down_near = call(
        fetch_kernel,
        (near(expert_gate_up.shape, BF16), near(expert_down.shape, BF16)),
        expert_gate_up, expert_down,
        hbm=(0, 1),
        scratch=[pltpu.SemaphoreType.DMA((4,))],
        name="fetch",
    )
    own, gu_near, down_near = lax.optimization_barrier((own, gu_near, down_near))
    devices = seq_n * exp_n
    slots = devices * 8
    half = model // 2
    order = exchange_order(seq_n, exp_n)
    experts_at = np.repeat(2 * np.asarray(order, np.int32), 8).reshape(1, slots)
    experts_at = experts_at + (np.arange(slots, dtype=np.int32) // 4 % 2)
    hidden_mid, normed, send, pick = call(
        route_kernel,
        (free((rows, model), BF16), piece, near((slots, half), BF16), near((4 * rows, slots), BF16)),
        own, got[1], got[2], got[3], residual, post_gain.reshape(1, model), route_ids.T, route_weight.T, jnp.asarray(experts_at),
        flops=2 * 10**8,
        name="route",
    )
    axes = ("seq", "exp")
    recv = lax.all_to_all(send.reshape(devices, 8, half), axes, split_axis=0, concat_axis=0, tiled=True, axis_index_groups=[order])
    made = call(
        expert_kernel,
        (far((slots, half), BF16),),
        recv.reshape(slots, half), gu_near, down_near,
        scratch=[
            pltpu.VMEM((half // 128, slots, 128), F32),
            pltpu.VMEM((half // 128, slots, 128), F32),
            pltpu.VMEM((2 * devices, model), BF16),
            pltpu.VMEM((2 * devices, model), BF16),
            pltpu.VMEM((slots, half), BF16),
            pltpu.SemaphoreType.DMA((half // 256,)),
        ],
        flops=4 * 10**9,
        name="experts",
    )
    made, normed = lax.optimization_barrier((made, normed))
    shared = call(
        shared_kernel,
        (near((rows, model), F32),),
        normed, shared_gate.reshape(1, model), shared_gate_up, shared_down,
        hbm=(2, 3),
        scratch=[
            pltpu.VMEM(shared_gate_up.shape, BF16),
            pltpu.VMEM(shared_down.shape, BF16),
            pltpu.SemaphoreType.DMA((2,)),
        ],
        flops=2 * 10**8,
        name="shared",
    )
    back = lax.all_to_all(made.reshape(devices, 8, half), axes, split_axis=0, concat_axis=0, tiled=True, axis_index_groups=[order])
    moe_out = call(
        combine_kernel,
        (free((rows, model), BF16),),
        back.reshape(slots, half), pick, shared,
        flops=3 * 10**8,
        name="combine",
    )
    return hidden_mid, moe_out


def solution(mesh):
    placed = (
        P("seq", None, "exp"),
        P("seq", "exp"),
        P("seq", "exp"),
        P(None, None, "exp"),
        P(None, "exp"),
        P("exp", "seq"),
        P("exp", "seq"),
        P(),
        P(),
        P("exp", None),
        P(("seq", "exp"), None),
        P(),
        P(("seq", "exp"), None),
        P(("seq", "exp"), None),
        P(("seq", "exp"), None, None, None),
        P(("seq", "exp"), None, None),
        P(),
        P(),
        P(),
    )
    return jax.shard_map(
        shards,
        mesh=mesh,
        in_specs=placed,
        out_specs=(P(("seq", "exp"), None), P(("seq", "exp"), None)),
        check_vma=False,
    )
```
